32 devices in a mesh: rep: 2 (over x), seq: 8 (over z, y), head: 2 (over core).
Axes of the slice: x: 2, y: 2, z: 4, core: 2. Of those that a mesh axis runs over, the one named last changes fastest.
Arguments:
- query_rows: bfloat16 [2048, 4096], P(('rep', 'seq'), 'head'), parts along dimension 0, may hold values from -40 to 40
- key_rows: bfloat16 [2048, 4096], P(('rep', 'seq'), 'head'), parts along dimension 0, may hold values from -6 to 6
- value_rows: bfloat16 [2048, 4096], P(('rep', 'seq'), 'head'), parts along dimension 0, may hold values from -6 to 6
- rand_blocks: int32 [16, 32, 3], P('rep'), parts along dimension 0, may hold values from 0 to 7, as said below
- out_weight: bfloat16 [4096, 4096], P('seq', 'head'), may hold values from -0.09375 to 0.09375
Outputs:
- projected: bfloat16 [2048, 4096], P(('rep', 'seq'), 'head'), parts along dimension 0
The draws below stay inside these ranges and needn't reach their ends.
There are 2 independent parts, one for each index of `rep`. The reference program is written for one: setup_inputs(seed, part) draws one part's arguments, and reference() takes and returns one part's arrays. A program takes and returns all parts, laid end to end along the dimension named above; an argument that names none is the same for every part. Nothing has to cross between parts.
Inputs may be any that keep to these rules, and one draw needn't show every extreme that they name: `rand_blocks`: each entry is uniform over the blocks of the whole sequence. For the query blocks of one index of seq and the heads of one index of head, at most 6 entries name blocks held by one index of seq, and in every draw some index of seq is named exactly 6 times.
All inputs are finite; a program needn't handle non-finite values.
Results may differ from the reference program's by a relative error of at most 0.008.
Values may be sent and summed in bfloat16 or wider, within the bound.
No kernel may reach another device: no remote copies, remote signals or barrier semaphores. Data moves between devices by JAX's collectives and lax.ppermute only.
A program may use at most 128 MiB of HBM per device.

```python
import math
import jax
import jax.numpy as jnp
from jax import lax

H = 32
HD = 128
DM = 4096
BLK = 128
R = 3
TOK_DEV = 128
TOKENS = 1024
NB = 8
N_SEQ = 8
N_HEAD = 2


def draw_query_rows(key, part):
    drawn = 3.0 * jax.random.truncated_normal(jax.random.fold_in(key, 103), -6.0, 6.0, (TOKENS, H * HD), jnp.float32)
    return drawn.astype(jnp.bfloat16)


def draw_key_rows(key, part):
    drawn = jax.random.truncated_normal(jax.random.fold_in(key, 104), -6.0, 6.0, (TOKENS, H * HD), jnp.float32)
    return drawn.astype(jnp.bfloat16)


def draw_rand_blocks(key, part):
    per_device = TOK_DEV // BLK
    group_heads = H // N_HEAD
    request_count = per_device * group_heads * R
    order_keys = jax.random.randint(jax.random.fold_in(key, 201), (N_SEQ, N_HEAD, N_SEQ), 0, 1 << 20) * N_SEQ + jnp.arange(N_SEQ)
    owner_order = jnp.argsort(order_keys, axis=2).astype(jnp.int32)
    owners = owner_order[:, :, jnp.arange(request_count) % N_SEQ]
    inner = jax.random.randint(jax.random.fold_in(key, 202), (N_SEQ, N_HEAD, request_count), 0, per_device)
    chosen_ids = owners * per_device + inner
    chosen_ids = chosen_ids.reshape(N_SEQ, N_HEAD, per_device, group_heads, R).transpose(0, 2, 1, 3, 4)
    return chosen_ids.reshape(NB, H, R).astype(jnp.int32)


def block_levels(stream_key, dims, shards, low, high):
    gain = 1.0
    for dim, shards_of in shards:
        draws = jax.random.uniform(jax.random.fold_in(jax.random.fold_in(stream_key, 6), dim), (shards_of,), jnp.float32, low / len(shards), high / len(shards))
        gain = gain * jnp.repeat(jnp.exp(draws), dims[dim] // shards_of).reshape((-1,) + (1,) * (len(dims) - 1 - dim))
    return gain


def noise(stream_key, dims, scale, most, shards=(), kind=jnp.bfloat16):
    factor_of = block_levels(stream_key, dims, shards, -0.22, 0.18) if shards else 1.0
    entries = jax.random.normal(stream_key, dims, jnp.float32) * scale * factor_of
    return jnp.minimum(jnp.maximum(entries, -most), most).astype(kind)


def setup_inputs(seed: int = 0, part: int = 0) -> dict:
    arg_keys = jax.random.split(jax.random.key(seed), 6)
    part_splits = jax.random.split(jax.random.fold_in(arg_keys[5], part), 6)
    return {
        "query_rows": draw_query_rows(jax.random.fold_in(jax.random.fold_in(arg_keys[5], part), 71), part),
        "key_rows": draw_key_rows(jax.random.fold_in(jax.random.fold_in(arg_keys[5], part), 71), part),
        "value_rows": noise(part_splits[2], (TOKENS, H * HD), 1.0, 6.0, ((0, 8), (1, 2))),
        "rand_blocks": draw_rand_blocks(jax.random.fold_in(jax.random.fold_in(arg_keys[5], part), 71), part),
        "out_weight": noise(arg_keys[4], (DM, H * HD), (H * HD) ** -0.5, 0.09375, ((0, 8), (1, 2))),
    }


def masked_softmax(scores, allowed):
    masked = jnp.where(allowed, scores, -jnp.inf)
    row_peak = lax.optimization_barrier(jnp.max(masked, axis=-1, keepdims=True))
    expon_terms = jnp.where(allowed, jnp.exp(masked - row_peak), 0.0)
    return expon_terms / lax.optimization_barrier(jnp.sum(expon_terms, axis=-1, keepdims=True))

def reference(query_rows, key_rows, value_rows, rand_blocks, out_weight):
    features = H * HD
    block_count = TOKENS // BLK
    score_scale = 1.0 / math.sqrt(HD)
    block_ids = jnp.arange(block_count, dtype=jnp.int32)
    base_slots = jnp.stack([jnp.zeros((block_count,), jnp.int32), jnp.full((block_count,), block_count - 1, jnp.int32), jnp.clip(block_ids - 1, 0, block_count - 1), block_ids, jnp.clip(block_ids + 1, 0, block_count - 1)], axis=1)
    slot_ids = jnp.concatenate([jnp.broadcast_to(base_slots[:, None, :], (block_count, H, 5)), rand_blocks.astype(jnp.int32)], axis=2)
    slot_count = slot_ids.shape[2]
    equal_pair = slot_ids[:, :, :, None] == slot_ids[:, :, None, :]
    earlier = jnp.arange(slot_count)[None, :] < jnp.arange(slot_count)[:, None]
    slot_live = jnp.logical_not(jnp.any(equal_pair & earlier[None, None], axis=3))
    query_blocks = query_rows.reshape(block_count, BLK, H, HD)
    key_blocks = key_rows.reshape(block_count, BLK, H, HD)
    value_blocks = value_rows.reshape(block_count, BLK, H, HD)
    head_column = jnp.arange(H, dtype=jnp.int32)[:, None]

    def one_block(block_items):
        query_here, chosen_ids, live_here = block_items
        keys_sel = key_blocks[chosen_ids, :, head_column, :].reshape(H, slot_count * BLK, HD).astype(jnp.float32)
        values_sel = value_blocks[chosen_ids, :, head_column, :].reshape(H, slot_count * BLK, HD).astype(jnp.float32)
        scores = jnp.einsum('bhd,hkd->hbk', query_here.astype(jnp.float32), keys_sel) * score_scale
        key_live = jnp.repeat(live_here, BLK, axis=1)
        weights = masked_softmax(scores, key_live[:, None, :]).astype(jnp.bfloat16)
        mixed = jnp.einsum('hbk,hkd->bhd', weights.astype(jnp.float32), values_sel)
        return mixed.astype(jnp.bfloat16)
    block_out = lax.map(one_block, (query_blocks, slot_ids, slot_live)).reshape(TOKENS, features)
    glob_query = jnp.concatenate((query_rows[:BLK], query_rows[TOKENS - BLK:]), axis=0)
    glob_query = glob_query.reshape(2 * BLK, H, HD).transpose(1, 0, 2)
    key_heads = key_rows.reshape(TOKENS, H, HD).transpose(1, 0, 2)
    value_heads = value_rows.reshape(TOKENS, H, HD).transpose(1, 0, 2)

    def one_head(head_items):
        query_head, key_head, value_head = head_items
        scores = jnp.dot(query_head, key_head.T, preferred_element_type=jnp.float32) * score_scale
        row_peak = lax.optimization_barrier(jnp.max(scores, axis=1, keepdims=True))
        expon_terms = jnp.exp(scores - row_peak)
        numer_terms = jnp.dot(expon_terms, value_head.astype(jnp.float32), preferred_element_type=jnp.float32)
        return (numer_terms / lax.optimization_barrier(jnp.sum(expon_terms, axis=1, keepdims=True))).astype(jnp.bfloat16)
    glob_out = lax.map(one_head, (glob_query, key_heads, value_heads))
    glob_out = glob_out.transpose(1, 0, 2).reshape(2 * BLK, features)
    attended = block_out.at[:BLK].set(glob_out[:BLK])
    attended = attended.at[TOKENS - BLK:].set(glob_out[BLK:])
    group_width = features // N_HEAD
    summed = jnp.zeros((TOKENS, DM), jnp.float32)
    for group_index in range(N_HEAD):
        part_in = attended[:, group_index * group_width:(group_index + 1) * group_width]
        weight_part = out_weight[:, group_index * group_width:(group_index + 1) * group_width]
        partial_out = lax.dot_general(part_in, weight_part, (((1,), (1,)), ((), ())), preferred_element_type=jnp.float32).astype(jnp.bfloat16)
        summed = summed + partial_out.astype(jnp.float32)
    return summed.astype(jnp.bfloat16)
```

```python
import math

import jax
import jax.numpy as jnp
from jax import lax
from jax.experimental import pallas as pl
from jax.experimental.pallas import tpu as pltpu
from jax.sharding import PartitionSpec as P

HD = 128
BLK = 128
R = 3
VMEM = 48 << 20


def broadcast(block, axis, owner):
    block = jnp.where(lax.axis_index(axis) == owner, block, jnp.zeros_like(block))
    return lax.psum(block, axis)


def padded(array, sides, width):
    for axis, dim in sides:
        peers, length = (lax.axis_size(axis), array.shape[dim])
        up = [(i, (i + 1) % peers) for i in range(peers - 1)]
        down = [(j, i) for i, j in up]
        last = lax.slice_in_dim(array, length - width, length, axis=dim)
        initial = lax.slice_in_dim(array, 0, width, axis=dim)
        before = lax.ppermute(last, axis, up)
        after = lax.ppermute(initial, axis, down)
        array = jnp.concatenate([before, array, after], axis=dim)
    return array


def masked_softmax(scores, allowed):
    masked = jnp.where(allowed, scores, -jnp.inf)
    row_peak = jnp.max(masked, axis=-1, keepdims=True)
    expon_terms = jnp.where(allowed, jnp.exp(masked - row_peak), 0.0)
    return expon_terms / jnp.sum(expon_terms, axis=-1, keepdims=True)


def share_block(stacked, root_index):
    return broadcast(stacked, "seq", root_index)


def local_by_rows(query_rows, key_rows, value_rows, rand_blocks, out_weight):
    tokens, features = query_rows.shape
    head_width = HD
    head_count = features // head_width
    blocks = tokens // BLK
    seq_count = lax.axis_size("seq")
    seq_index = lax.axis_index("seq")
    head_index = lax.axis_index("head")
    block_total = blocks * seq_count
    score_scale = 1.0 / math.sqrt(head_width)
    request_count = blocks * head_count * R
    slot_depth = (request_count + seq_count - 1) // seq_count
    first_rows = jnp.stack((query_rows, key_rows, value_rows))
    final_rows = jnp.stack((query_rows, key_rows, value_rows))
    first_glob = share_block(first_rows, 0)
    final_glob = share_block(final_rows, seq_count - 1)
    paired = jnp.stack((key_rows, value_rows))
    extended = padded(paired, (("seq", 1),), BLK)
    ext_heads = extended.reshape(2, blocks + 2, BLK, head_count, head_width).transpose(
        0, 3, 1, 2, 4
    )
    group_table = lax.dynamic_slice_in_dim(rand_blocks, head_index * head_count, head_count, 1)
    all_requests = group_table.reshape(seq_count, request_count)
    all_owner = all_requests // blocks
    request_order = jnp.arange(request_count, dtype=jnp.int32)
    earlier_request = request_order[None, :] < request_order[:, None]
    same_owner = all_owner[:, :, None] == all_owner[:, None, :]
    all_position = jnp.sum(same_owner & earlier_request[None], axis=2)
    owned_here = all_owner == seq_index
    slot_range = jnp.arange(slot_depth, dtype=jnp.int32)
    picked = owned_here[:, None, :] & (all_position[:, None, :] == slot_range[None, :, None])
    picked_request = jnp.sum(jnp.where(picked, request_order[None, None, :], 0), axis=2)
    picked_block = jnp.take_along_axis(all_requests, picked_request, axis=1) - seq_index * blocks
    picked_block = jnp.clip(picked_block, 0, blocks - 1).reshape(-1)
    picked_head = (picked_request // R % head_count).reshape(-1)
    local_pairs = paired.reshape(2, blocks, BLK, head_count, head_width)
    outgoing = local_pairs[:, picked_block, :, picked_head, :]
    outgoing = outgoing.reshape(seq_count, slot_depth, 2, BLK, head_width)
    received = lax.all_to_all(outgoing, "seq", split_axis=0, concat_axis=0, tiled=True)
    my_requests = lax.dynamic_slice_in_dim(all_requests, seq_index, 1, 0)[0]
    my_position = lax.dynamic_slice_in_dim(all_position, seq_index, 1, 0)[0]
    my_owner = my_requests // blocks
    rand_pairs = jnp.take(
        received.reshape(seq_count * slot_depth, 2, BLK, head_width),
        my_owner * slot_depth + my_position,
        axis=0,
    )
    rand_pairs = rand_pairs.reshape(blocks, head_count, R, 2, BLK, head_width).transpose(
        3, 1, 0, 2, 4, 5
    )
    block_ids = seq_index * blocks + jnp.arange(blocks, dtype=jnp.int32)
    base_slots = jnp.stack(
        [
            jnp.zeros((blocks,), jnp.int32),
            jnp.full((blocks,), block_total - 1, jnp.int32),
            jnp.clip(block_ids - 1, 0, block_total - 1),
            block_ids,
            jnp.clip(block_ids + 1, 0, block_total - 1),
        ],
        axis=1,
    )
    my_table = my_requests.reshape(blocks, head_count, R).transpose(1, 0, 2)
    slot_ids = jnp.concatenate(
        [jnp.broadcast_to(base_slots[None], (head_count, blocks, 5)), my_table], axis=2
    )
    slot_count = slot_ids.shape[2]
    equal_pair = slot_ids[:, :, :, None] == slot_ids[:, :, None, :]
    earlier = jnp.arange(slot_count)[None, :] < jnp.arange(slot_count)[:, None]
    slot_live = jnp.logical_not(jnp.any(equal_pair & earlier[None, None], axis=3))
    key_live = jnp.repeat(slot_live, BLK, axis=2)
    window_index = jnp.arange(blocks)[:, None] + jnp.arange(3)[None, :]
    query_heads = query_rows.reshape(blocks, BLK, head_count, head_width).transpose(2, 0, 1, 3)
    first_heads = first_glob.reshape(3, BLK, head_count, head_width).transpose(0, 2, 1, 3)
    final_heads = final_glob.reshape(3, BLK, head_count, head_width).transpose(0, 2, 1, 3)
    target_heads = max(1, 512 // (blocks * BLK))
    heads_step = max(
        (
            width
            for width in range(1, head_count + 1)
            if head_count % width == 0 and width <= target_heads
        )
    )

    def collect(ext_part, first_block, final_block, rand_part):
        steps_here = ext_part.shape[0]
        window_blocks = ext_part[:, window_index]
        glob_blocks = jnp.stack((first_block, final_block), axis=1)[:, None]
        joined = jnp.concatenate([glob_blocks, window_blocks, rand_part], axis=2)
        return joined.reshape(steps_here, blocks, slot_count * BLK, head_width)

    def attend(head_items):
        (
            query_one,
            key_ext,
            value_ext,
            key_first,
            value_first,
            key_final,
            value_final,
            key_rand,
            value_rand,
            live_one,
        ) = head_items
        keys_sel = collect(key_ext, key_first, key_final, key_rand)
        values_sel = collect(value_ext, value_first, value_final, value_rand)
        scores = (
            jnp.einsum("hibd,hikd->hibk", query_one, keys_sel, preferred_element_type=jnp.float32)
            * score_scale
        )
        weights = masked_softmax(scores, live_one[:, :, None, :]).astype(jnp.bfloat16)
        mixed = jnp.einsum(
            "hibk,hikd->hibd", weights, values_sel, preferred_element_type=jnp.float32
        )
        return mixed.astype(jnp.bfloat16)

    def split_heads(array):
        return array.reshape((head_count // heads_step, heads_step) + array.shape[1:])

    head_inputs = (
        query_heads,
        ext_heads[0],
        ext_heads[1],
        first_heads[1],
        first_heads[2],
        final_heads[1],
        final_heads[2],
        rand_pairs[0],
        rand_pairs[1],
        key_live,
    )
    block_heads = lax.map(attend, tuple((split_heads(item) for item in head_inputs)))
    block_heads = block_heads.reshape(head_count, blocks, BLK, head_width)
    attended = block_heads.transpose(1, 2, 0, 3).reshape(tokens, features)
    glob_query = jnp.concatenate((first_glob[0], final_glob[0]), axis=0).reshape(
        2 * BLK, head_count, head_width
    )
    key_heads = key_rows.reshape(tokens, head_count, head_width)
    value_wide = value_rows.reshape(tokens, head_count, head_width).astype(jnp.float32)
    glob_scores = (
        jnp.einsum("rhd,thd->hrt", glob_query, key_heads, preferred_element_type=jnp.float32)
        * score_scale
    )
    local_peak = jnp.max(glob_scores, axis=2)
    row_peak = lax.pmax(local_peak, "seq")
    expon_terms = jnp.exp(glob_scores - row_peak[:, :, None])
    denoms = jnp.sum(expon_terms, axis=2)
    numer_terms = jnp.einsum(
        "hrt,thd->hrd", expon_terms, value_wide, preferred_element_type=jnp.float32
    )
    numer_terms, denoms = lax.psum((numer_terms, denoms), "seq")
    glob_out = (
        (numer_terms / denoms[:, :, None])
        .astype(jnp.bfloat16)
        .transpose(1, 0, 2)
        .reshape(2 * BLK, features)
    )
    head_block = jnp.where(seq_index == 0, glob_out[:BLK], attended)
    attended = attended.at[:BLK].set(head_block)
    tail_block = jnp.where(seq_index == seq_count - 1, glob_out[BLK:], attended)
    attended = attended.at[tokens - BLK :].set(tail_block)
    partial_terms = lax.dot_general(
        lax.all_gather(out_weight, "seq", axis=0, tiled=True),
        attended,
        (((1,), (1,)), ((), ())),
        preferred_element_type=jnp.float32,
    )
    summed = lax.psum_scatter(
        partial_terms.astype(jnp.bfloat16), "head", scatter_dimension=0, tiled=True
    ).astype(jnp.float32)
    return summed.T.astype(jnp.bfloat16)


def spread_kernel(query_ref, key_ref, value_ref, out_ref):
    out_ref[0, 0] = query_ref[...]
    out_ref[0, 1] = key_ref[...]
    out_ref[0, 2] = value_ref[...]


def spread(query_rows, key_rows, value_rows, peers):
    tokens, features = query_rows.shape
    width = features // peers
    rows = pl.BlockSpec((tokens, width), lambda j: (0, j))
    return pl.pallas_call(
        spread_kernel,
        grid=(peers,),
        in_specs=[rows] * 3,
        out_specs=pl.BlockSpec((1, 3, tokens, width), lambda j: (j, 0, 0, 0)),
        out_shape=jax.ShapeDtypeStruct((peers, 3, tokens, width), query_rows.dtype),
    )(query_rows, key_rows, value_rows)


def attend_kernel(query_ref, key_ref, value_ref, bias_ref, out_ref):
    groups, _, tokens, width = query_ref.shape
    total = groups * tokens
    blocks = total // BLK
    factor = math.log2(math.e) / math.sqrt(width)
    keys = key_ref[...].reshape(total, width)
    values = value_ref[...].reshape(total, width)
    query = query_ref[...].reshape(total, width)
    for block in range(blocks):
        rows = slice(block * BLK, (block + 1) * BLK)
        scores = lax.dot_general(
            query[rows], keys, (((1,), (1,)), ((), ())), preferred_element_type=jnp.float32
        )
        scores = scores * factor + bias_ref[0, block : block + 1, :]
        peak = jnp.max(scores, axis=1, keepdims=True)
        terms = jnp.exp2(scores - peak)
        denom = jnp.sum(terms, axis=1, keepdims=True)
        mixed = jnp.dot(
            terms.astype(jnp.bfloat16), values, preferred_element_type=jnp.float32
        )
        out_ref[rows, :] = (mixed / denom).astype(out_ref.dtype)


def attend_heads(rows, bias):
    groups, _, tokens, features = rows.shape
    heads = features // HD
    total = groups * tokens

    def part(which):
        return pl.BlockSpec((groups, 1, tokens, HD), lambda h: (0, which, 0, h))

    return pl.pallas_call(
        attend_kernel,
        grid=(heads,),
        in_specs=[
            part(0),
            part(1),
            part(2),
            pl.BlockSpec((1,) + bias.shape[1:], lambda h: (h, 0, 0)),
        ],
        out_specs=pl.BlockSpec((total, HD), lambda h: (0, h)),
        out_shape=jax.ShapeDtypeStruct((total, features), rows.dtype),
        compiler_params=pltpu.CompilerParams(vmem_limit_bytes=VMEM),
    )(rows, rows, rows, bias)


def project_kernel(head_ref, rows_ref, weight_ref, send_ref, keep_ref, total_ref):
    step = pl.program_id(0)
    half = send_ref.shape[1]

    @pl.when(step == 0)
    def _():
        total_ref[...] = jnp.zeros_like(total_ref)

    total_ref[...] += lax.dot_general(
        rows_ref[0],
        weight_ref[...],
        (((1,), (1,)), ((), ())),
        preferred_element_type=jnp.float32,
    )

    @pl.when(step == pl.num_programs(0) - 1)
    def _():
        low = total_ref[:, :half].astype(send_ref.dtype)
        high = total_ref[:, half:].astype(send_ref.dtype)
        first = head_ref[0] == 0
        send_ref[...] = jnp.where(first, high, low)
        keep_ref[...] = jnp.where(first, low, high)


def project(head, gathered, weight):
    peers, total, width = gathered.shape
    outs = weight.shape[0]
    half = outs // 2
    result = jax.ShapeDtypeStruct((total, half), gathered.dtype)
    whole = pl.BlockSpec((total, half), lambda j, _: (0, 0))
    return pl.pallas_call(
        project_kernel,
        grid_spec=pltpu.PrefetchScalarGridSpec(
            num_scalar_prefetch=1,
            grid=(peers,),
            in_specs=[
                pl.BlockSpec((1, total, width), lambda j, _: (j, 0, 0)),
                pl.BlockSpec((outs, width), lambda j, _: (0, j)),
            ],
            out_specs=[whole, whole],
            scratch_shapes=[pltpu.VMEM((total, outs), jnp.float32)],
        ),
        out_shape=[result, result],
        compiler_params=pltpu.CompilerParams(vmem_limit_bytes=VMEM),
    )(head, gathered, weight)


def key_bias(rand_blocks, head_start, heads):
    block_total = rand_blocks.shape[0]
    ids = jnp.arange(block_total, dtype=jnp.int32)
    near = jnp.abs(ids[:, None] - ids[None, :]) <= 1
    ends = (ids == 0) | (ids == block_total - 1)
    fixed = near | ends[None, :] | ends[:, None]
    chosen = lax.dynamic_slice_in_dim(rand_blocks, head_start, heads, 1)
    named = jnp.any(chosen[:, :, :, None] == ids, axis=2).transpose(1, 0, 2)
    live = named | fixed[None]
    return jnp.repeat(jnp.where(live, 0.0, -1e30).astype(jnp.float32), BLK, axis=2)


def local_by_heads(query_rows, key_rows, value_rows, rand_blocks, out_weight):
    tokens, features = query_rows.shape
    peers = lax.axis_size("seq")
    seq_index = lax.axis_index("seq")
    head_index = lax.axis_index("head")
    heads = features // HD // peers
    outgoing = spread(query_rows, key_rows, value_rows, peers)
    rows = lax.all_to_all(outgoing, "seq", split_axis=0, concat_axis=0, tiled=True)
    bias = key_bias(rand_blocks, head_index * (features // HD) + seq_index * heads, heads)
    attended = attend_heads(rows, bias)
    gathered = lax.all_gather(attended, "seq", axis=0)
    swap = [(0, 1), (1, 0)]
    send, keep = project(head_index[None], gathered, out_weight)
    other = lax.ppermute(send, "head", swap)
    summed = (keep.astype(jnp.float32) + other.astype(jnp.float32)).astype(jnp.bfloat16)
    outs = summed.shape[1]
    summed = summed.reshape(peers, tokens, outs)
    arrived = lax.all_to_all(summed, "seq", split_axis=0, concat_axis=0, tiled=True)
    arrived = arrived.reshape(2, peers // 2, tokens, outs)
    mine = lax.dynamic_index_in_dim(arrived, head_index, 0, keepdims=False)
    theirs = lax.dynamic_index_in_dim(arrived, 1 - head_index, 0, keepdims=False)
    crossed = lax.ppermute(theirs, "head", swap)
    first = head_index == 0
    pair = jnp.stack(
        [jnp.where(first, mine, crossed), jnp.where(first, crossed, mine)], axis=1
    )
    return pair.transpose(2, 0, 1, 3).reshape(tokens, features)


def local(query_rows, key_rows, value_rows, rand_blocks, out_weight):
    head_count = query_rows.shape[1] // HD
    peers = lax.axis_size("seq")
    if lax.axis_size("head") == 2 and head_count % peers == 0 and peers % 2 == 0:
        return local_by_heads(query_rows, key_rows, value_rows, rand_blocks, out_weight)
    return local_by_rows(query_rows, key_rows, value_rows, rand_blocks, out_weight)


def solution(mesh):
    placed = (
        P(("rep", "seq"), "head"),
        P(("rep", "seq"), "head"),
        P(("rep", "seq"), "head"),
        P("rep", None, None),
        P("seq", "head"),
    )
    return jax.shard_map(
        local, mesh=mesh, in_specs=placed, out_specs=P(("rep", "seq"), "head"), check_vma=False
    )
```

```python
import functools
import math

import jax
import jax.numpy as jnp
from jax import lax
from jax.experimental import pallas as pl
from jax.experimental.pallas import tpu as pltpu
from jax.sharding import PartitionSpec as P

HD = 128
BLK = 128
R = 3
VMEM = 20 << 20
TILE = 256
EARLY = 6


def broadcast(block, axis, owner):
    block = jnp.where(lax.axis_index(axis) == owner, block, jnp.zeros_like(block))
    return lax.psum(block, axis)


def padded(array, sides, width):
    for axis, dim in sides:
        peers, length = (lax.axis_size(axis), array.shape[dim])
        up = [(i, (i + 1) % peers) for i in range(peers - 1)]
        down = [(j, i) for i, j in up]
        last = lax.slice_in_dim(array, length - width, length, axis=dim)
        initial = lax.slice_in_dim(array, 0, width, axis=dim)
        before = lax.ppermute(last, axis, up)
        after = lax.ppermute(initial, axis, down)
        array = jnp.concatenate([before, array, after], axis=dim)
    return array


def masked_softmax(scores, allowed):
    masked = jnp.where(allowed, scores, -jnp.inf)
    row_peak = jnp.max(masked, axis=-1, keepdims=True)
    expon_terms = jnp.where(allowed, jnp.exp(masked - row_peak), 0.0)
    return expon_terms / jnp.sum(expon_terms, axis=-1, keepdims=True)


def share_block(stacked, root_index):
    return broadcast(stacked, "seq", root_index)


def local_by_rows(query_rows, key_rows, value_rows, rand_blocks, out_weight):
    tokens, features = query_rows.shape
    head_width = HD
    head_count = features // head_width
    blocks = tokens // BLK
    seq_count = lax.axis_size("seq")
    seq_index = lax.axis_index("seq")
    head_index = lax.axis_index("head")
    block_total = blocks * seq_count
    score_scale = 1.0 / math.sqrt(head_width)
    request_count = blocks * head_count * R
    slot_depth = (request_count + seq_count - 1) // seq_count
    first_rows = jnp.stack((query_rows, key_rows, value_rows))
    final_rows = jnp.stack((query_rows, key_rows, value_rows))
    first_glob = share_block(first_rows, 0)
    final_glob = share_block(final_rows, seq_count - 1)
    paired = jnp.stack((key_rows, value_rows))
    extended = padded(paired, (("seq", 1),), BLK)
    ext_heads = extended.reshape(2, blocks + 2, BLK, head_count, head_width).transpose(
        0, 3, 1, 2, 4
    )
    group_table = lax.dynamic_slice_in_dim(rand_blocks, head_index * head_count, head_count, 1)
    all_requests = group_table.reshape(seq_count, request_count)
    all_owner = all_requests // blocks
    request_order = jnp.arange(request_count, dtype=jnp.int32)
    earlier_request = request_order[None, :] < request_order[:, None]
    same_owner = all_owner[:, :, None] == all_owner[:, None, :]
    all_position = jnp.sum(same_owner & earlier_request[None], axis=2)
    owned_here = all_owner == seq_index
    slot_range = jnp.arange(slot_depth, dtype=jnp.int32)
    picked = owned_here[:, None, :] & (all_position[:, None, :] == slot_range[None, :, None])
    picked_request = jnp.sum(jnp.where(picked, request_order[None, None, :], 0), axis=2)
    picked_block = jnp.take_along_axis(all_requests, picked_request, axis=1) - seq_index * blocks
    picked_block = jnp.clip(picked_block, 0, blocks - 1).reshape(-1)
    picked_head = (picked_request // R % head_count).reshape(-1)
    local_pairs = paired.reshape(2, blocks, BLK, head_count, head_width)
    outgoing = local_pairs[:, picked_block, :, picked_head, :]
    outgoing = outgoing.reshape(seq_count, slot_depth, 2, BLK, head_width)
    received = lax.all_to_all(outgoing, "seq", split_axis=0, concat_axis=0, tiled=True)
    my_requests = lax.dynamic_slice_in_dim(all_requests, seq_index, 1, 0)[0]
    my_position = lax.dynamic_slice_in_dim(all_position, seq_index, 1, 0)[0]
    my_owner = my_requests // blocks
    rand_pairs = jnp.take(
        received.reshape(seq_count * slot_depth, 2, BLK, head_width),
        my_owner * slot_depth + my_position,
        axis=0,
    )
    rand_pairs = rand_pairs.reshape(blocks, head_count, R, 2, BLK, head_width).transpose(
        3, 1, 0, 2, 4, 5
    )
    block_ids = seq_index * blocks + jnp.arange(blocks, dtype=jnp.int32)
    base_slots = jnp.stack(
        [
            jnp.zeros((blocks,), jnp.int32),
            jnp.full((blocks,), block_total - 1, jnp.int32),
            jnp.clip(block_ids - 1, 0, block_total - 1),
            block_ids,
            jnp.clip(block_ids + 1, 0, block_total - 1),
        ],
        axis=1,
    )
    my_table = my_requests.reshape(blocks, head_count, R).transpose(1, 0, 2)
    slot_ids = jnp.concatenate(
        [jnp.broadcast_to(base_slots[None], (head_count, blocks, 5)), my_table], axis=2
    )
    slot_count = slot_ids.shape[2]
    equal_pair = slot_ids[:, :, :, None] == slot_ids[:, :, None, :]
    earlier = jnp.arange(slot_count)[None, :] < jnp.arange(slot_count)[:, None]
    slot_live = jnp.logical_not(jnp.any(equal_pair & earlier[None, None], axis=3))
    key_live = jnp.repeat(slot_live, BLK, axis=2)
    window_index = jnp.arange(blocks)[:, None] + jnp.arange(3)[None, :]
    query_heads = query_rows.reshape(blocks, BLK, head_count, head_width).transpose(2, 0, 1, 3)
    first_heads = first_glob.reshape(3, BLK, head_count, head_width).transpose(0, 2, 1, 3)
    final_heads = final_glob.reshape(3, BLK, head_count, head_width).transpose(0, 2, 1, 3)
    target_heads = max(1, 512 // (blocks * BLK))
    heads_step = max(
        (
            width
            for width in range(1, head_count + 1)
            if head_count % width == 0 and width <= target_heads
        )
    )

    def collect(ext_part, first_block, final_block, rand_part):
        steps_here = ext_part.shape[0]
        window_blocks = ext_part[:, window_index]
        glob_blocks = jnp.stack((first_block, final_block), axis=1)[:, None]
        joined = jnp.concatenate([glob_blocks, window_blocks, rand_part], axis=2)
        return joined.reshape(steps_here, blocks, slot_count * BLK, head_width)

    def attend(head_items):
        (
            query_one,
            key_ext,
            value_ext,
            key_first,
            value_first,
            key_final,
            value_final,
            key_rand,
            value_rand,
            live_one,
        ) = head_items
        keys_sel = collect(key_ext, key_first, key_final, key_rand)
        values_sel = collect(value_ext, value_first, value_final, value_rand)
        scores = (
            jnp.einsum("hibd,hikd->hibk", query_one, keys_sel, preferred_element_type=jnp.float32)
            * score_scale
        )
        weights = masked_softmax(scores, live_one[:, :, None, :]).astype(jnp.bfloat16)
        mixed = jnp.einsum(
            "hibk,hikd->hibd", weights, values_sel, preferred_element_type=jnp.float32
        )
        return mixed.astype(jnp.bfloat16)

    def split_heads(array):
        return array.reshape((head_count // heads_step, heads_step) + array.shape[1:])

    head_inputs = (
        query_heads,
        ext_heads[0],
        ext_heads[1],
        first_heads[1],
        first_heads[2],
        final_heads[1],
        final_heads[2],
        rand_pairs[0],
        rand_pairs[1],
        key_live,
    )
    block_heads = lax.map(attend, tuple((split_heads(item) for item in head_inputs)))
    block_heads = block_heads.reshape(head_count, blocks, BLK, head_width)
    attended = block_heads.transpose(1, 2, 0, 3).reshape(tokens, features)
    glob_query = jnp.concatenate((first_glob[0], final_glob[0]), axis=0).reshape(
        2 * BLK, head_count, head_width
    )
    key_heads = key_rows.reshape(tokens, head_count, head_width)
    value_wide = value_rows.reshape(tokens, head_count, head_width).astype(jnp.float32)
    glob_scores = (
        jnp.einsum("rhd,thd->hrt", glob_query, key_heads, preferred_element_type=jnp.float32)
        * score_scale
    )
    local_peak = jnp.max(glob_scores, axis=2)
    row_peak = lax.pmax(local_peak, "seq")
    expon_terms = jnp.exp(glob_scores - row_peak[:, :, None])
    denoms = jnp.sum(expon_terms, axis=2)
    numer_terms = jnp.einsum(
        "hrt,thd->hrd", expon_terms, value_wide, preferred_element_type=jnp.float32
    )
    numer_terms, denoms = lax.psum((numer_terms, denoms), "seq")
    glob_out = (
        (numer_terms / denoms[:, :, None])
        .astype(jnp.bfloat16)
        .transpose(1, 0, 2)
        .reshape(2 * BLK, features)
    )
    head_block = jnp.where(seq_index == 0, glob_out[:BLK], attended)
    attended = attended.at[:BLK].set(head_block)
    tail_block = jnp.where(seq_index == seq_count - 1, glob_out[BLK:], attended)
    attended = attended.at[tokens - BLK :].set(tail_block)
    partial_terms = lax.dot_general(
        lax.all_gather(out_weight, "seq", axis=0, tiled=True),
        attended,
        (((1,), (1,)), ((), ())),
        preferred_element_type=jnp.float32,
    )
    summed = lax.psum_scatter(
        partial_terms.astype(jnp.bfloat16), "head", scatter_dimension=0, tiled=True
    ).astype(jnp.float32)
    return summed.T.astype(jnp.bfloat16)


def spread_kernel(query_ref, key_ref, value_ref, out_ref):
    peers, _, _, width = out_ref.shape
    for which, ref in enumerate((query_ref, key_ref, value_ref)):
        for peer in range(peers):
            out_ref[peer, which] = ref[:, peer * width : (peer + 1) * width]


def spread(query_rows, key_rows, value_rows, peers):
    tokens, features = query_rows.shape
    width = features // peers
    return pl.pallas_call(
        spread_kernel,
        out_shape=jax.ShapeDtypeStruct((peers, 3, tokens, width), query_rows.dtype),
        cost_estimate=pl.CostEstimate(
            flops=0, bytes_accessed=12 * tokens * features, transcendentals=0
        ),
    )(query_rows, key_rows, value_rows)


def attend_kernel(head, rows_ref, bias_ref, out_ref):
    groups, _, tokens, _ = rows_ref.shape
    total = groups * tokens
    blocks = total // BLK
    factor = math.log2(math.e) / math.sqrt(HD)
    lanes = slice(head * HD, (head + 1) * HD)
    query = rows_ref[:, 0, :, lanes].reshape(total, HD)
    keys = rows_ref[:, 1, :, lanes].reshape(total, HD)
    values = rows_ref[:, 2, :, lanes].reshape(total, HD)
    for block in range(blocks):
        rows = slice(block * BLK, (block + 1) * BLK)
        scores = lax.dot_general(
            query[rows], keys, (((1,), (1,)), ((), ())), preferred_element_type=jnp.float32
        )
        scores = scores * factor + bias_ref[head, block : block + 1, :]
        peak = jnp.max(scores, axis=1, keepdims=True)
        terms = jnp.exp2(scores - peak)
        denom = jnp.sum(terms, axis=1, keepdims=True)
        mixed = jnp.dot(
            terms.astype(jnp.bfloat16), values, preferred_element_type=jnp.float32
        )
        out_ref[rows, :] = (mixed / denom).astype(out_ref.dtype)


def attend_head(rows, bias, head):
    groups, _, tokens, _ = rows.shape
    total = groups * tokens
    return pl.pallas_call(
        functools.partial(attend_kernel, head),
        out_shape=jax.ShapeDtypeStruct((total, HD), rows.dtype),
        compiler_params=pltpu.CompilerParams(vmem_limit_bytes=VMEM),
        cost_estimate=pl.CostEstimate(
            flops=4 * total * total * HD,
            bytes_accessed=8 * total * HD,
            transcendentals=total * total,
        ),
    )(rows, bias)


def product_tile(owner_ref, pieces, weight_ref, tile):
    heads = len(pieces) // owner_ref.shape[0]
    width = heads * HD
    rows = jnp.concatenate([piece[tile, :] for piece in pieces], axis=1)
    columns = [
        weight_ref[:, pl.ds(pl.multiple_of(owner_ref[k] * width, width), width)]
        for k in range(owner_ref.shape[0])
    ]
    return lax.dot_general(
        rows,
        jnp.concatenate(columns, axis=1),
        (((1,), (1,)), ((), ())),
        preferred_element_type=jnp.float32,
    )


def early_kernel(owner_ref, weight_ref, *refs):
    *pieces, total_ref = refs
    for start in range(0, total_ref.shape[0], TILE):
        tile = slice(start, start + TILE)
        total_ref[tile, :] = product_tile(owner_ref, pieces, weight_ref, tile)


def late_kernel(owner_ref, side_ref, weight_ref, total_ref, *refs):
    *pieces, send_ref, keep_ref = refs
    half = send_ref.shape[1]
    for start in range(0, total_ref.shape[0], TILE):
        tile = slice(start, start + TILE)
        summed = total_ref[tile, :] + product_tile(owner_ref, pieces, weight_ref, tile)
        low = summed[:, :half].astype(send_ref.dtype)
        high = summed[:, half:].astype(send_ref.dtype)
        first = side_ref[0] == 0
        send_ref[tile, :] = jnp.where(first, high, low)
        keep_ref[tile, :] = jnp.where(first, low, high)


SCALARS = pl.BlockSpec(memory_space=pltpu.SMEM)
ARRAY = pl.BlockSpec(memory_space=pltpu.VMEM)


def project_early(owners, pieces, weight):
    total, width = pieces[0].shape
    outs = weight.shape[0]
    return pl.pallas_call(
        early_kernel,
        in_specs=[SCALARS] + [ARRAY] * (1 + len(pieces)),
        out_shape=jax.ShapeDtypeStruct((total, outs), jnp.float32),
        compiler_params=pltpu.CompilerParams(vmem_limit_bytes=VMEM),
        cost_estimate=pl.CostEstimate(
            flops=2 * total * outs * width * len(pieces),
            bytes_accessed=2 * len(pieces) * width * (total + outs) + 4 * total * outs,
            transcendentals=0,
        ),
    )(owners, weight, *pieces)


def project_late(owners, side, pieces, weight, so_far):
    total, width = pieces[0].shape
    outs = weight.shape[0]
    return pl.pallas_call(
        late_kernel,
        in_specs=[SCALARS] * 2 + [ARRAY] * (2 + len(pieces)),
        out_shape=[jax.ShapeDtypeStruct((total, outs // 2), pieces[0].dtype)] * 2,
        compiler_params=pltpu.CompilerParams(vmem_limit_bytes=VMEM),
        cost_estimate=pl.CostEstimate(
            flops=2 * total * outs * width * len(pieces),
            bytes_accessed=2 * len(pieces) * width * (total + outs) + 6 * total * outs,
            transcendentals=0,
        ),
    )(owners, side, weight, so_far, *pieces)


def key_bias(rand_blocks, head_start, heads):
    block_total = rand_blocks.shape[0]
    ids = jnp.arange(block_total, dtype=jnp.int32)
    near = jnp.abs(ids[:, None] - ids[None, :]) <= 1
    ends = (ids == 0) | (ids == block_total - 1)
    fixed = near | ends[None, :] | ends[:, None]
    chosen = lax.dynamic_slice_in_dim(rand_blocks, head_start, heads, 1)
    named = jnp.any(chosen[:, :, :, None] == ids, axis=2).transpose(1, 0, 2)
    live = named | fixed[None]
    return jnp.repeat(jnp.where(live, 0.0, -1e30).astype(jnp.float32), BLK, axis=2)


def ring_order(peers):
    return list(range(0, peers, 2)) + list(range(peers - 1, 0, -2))


def local_by_heads(query_rows, key_rows, value_rows, rand_blocks, out_weight):
    tokens, features = query_rows.shape
    peers = lax.axis_size("seq")
    seq_index = lax.axis_index("seq")
    head_index = lax.axis_index("head")
    heads = features // HD // peers
    order = ring_order(peers)
    onward = [(order[i], order[(i + 1) % peers]) for i in range(peers)]
    back = [(target, source) for source, target in onward]
    outgoing = spread(query_rows, key_rows, value_rows, peers)
    bias = key_bias(rand_blocks, head_index * (features // HD) + seq_index * heads, heads)
    reach = peers // 2
    far = {}
    rows = lax.all_to_all(outgoing, "seq", split_axis=0, concat_axis=0, tiled=True)
    for head in range(heads):
        mine = attend_head(rows, bias, head)
        ahead, behind = (mine, mine)
        far[head, 0] = mine
        for step in range(1, reach):
            ahead = lax.ppermute(ahead, "seq", onward)
            behind = lax.ppermute(behind, "seq", back)
            far[head, step] = ahead
            far[head, -step] = behind
        if head % 2 == 0:
            far[head, reach] = lax.ppermute(ahead, "seq", onward)
        else:
            far[head, reach] = lax.ppermute(behind, "seq", back)
    place = jnp.where(seq_index % 2 == 0, seq_index // 2, peers - (seq_index + 1) // 2)

    def gather_args(steps):
        spots = (place - jnp.array(steps, jnp.int32)) % peers
        owners = jnp.where(spots < reach, 2 * spots, 2 * (peers - spots) - 1)
        return owners, [far[head, step] for step in steps for head in range(heads)]

    steps = [0] + [step for hop in range(1, reach) for step in (hop, -hop)] + [reach]
    owners, pieces = gather_args(steps[:EARLY])
    so_far = project_early(owners, pieces, out_weight)
    owners, pieces = gather_args(steps[EARLY:])
    send, keep = project_late(owners, head_index[None], pieces, out_weight, so_far)
    swap = [(0, 1), (1, 0)]
    other = lax.ppermute(send, "head", swap)
    summed = (keep.astype(jnp.float32) + other.astype(jnp.float32)).astype(jnp.bfloat16)
    outs = summed.shape[1]
    summed = summed.reshape(peers, tokens, outs)
    arrived = lax.all_to_all(summed, "seq", split_axis=0, concat_axis=0, tiled=True)
    arrived = arrived.reshape(2, peers // 2, tokens, outs)
    mine = lax.dynamic_index_in_dim(arrived, head_index, 0, keepdims=False)
    theirs = lax.dynamic_index_in_dim(arrived, 1 - head_index, 0, keepdims=False)
    crossed = lax.ppermute(theirs, "head", swap)
    first = head_index == 0
    pair = jnp.stack(
        [jnp.where(first, mine, crossed), jnp.where(first, crossed, mine)], axis=1
    )
    return pair.transpose(2, 0, 1, 3).reshape(tokens, features)


def local(query_rows, key_rows, value_rows, rand_blocks, out_weight):
    head_count = query_rows.shape[1] // HD
    peers = lax.axis_size("seq")
    if lax.axis_size("head") == 2 and head_count % peers == 0 and peers % 2 == 0 and peers > 2:
        return local_by_heads(query_rows, key_rows, value_rows, rand_blocks, out_weight)
    return local_by_rows(query_rows, key_rows, value_rows, rand_blocks, out_weight)


def solution(mesh):
    placed = (
        P(("rep", "seq"), "head"),
        P(("rep", "seq"), "head"),
        P(("rep", "seq"), "head"),
        P("rep", None, None),
        P("seq", "head"),
    )
    return jax.shard_map(
        local, mesh=mesh, in_specs=placed, out_specs=P(("rep", "seq"), "head"), check_vma=False
    )
```

```python
import functools
import math

import jax
import jax.numpy as jnp
from jax import lax
from jax.experimental import pallas as pl
from jax.experimental.pallas import tpu as pltpu
from jax.sharding import PartitionSpec as P

HD = 128
BLK = 128
R = 3
VMEM = 20 << 20
TILE = 256
EARLY = 6
SEND_ORDER = (4, 6, 5, 7, 2, 3, 1)
SCALARS = pl.BlockSpec(memory_space=pltpu.SMEM)
ARRAY = pl.BlockSpec(memory_space=pltpu.VMEM)


def broadcast(block, axis, owner):
    block = jnp.where(lax.axis_index(axis) == owner, block, jnp.zeros_like(block))
    return lax.psum(block, axis)


def padded(array, sides, width):
    for axis, dim in sides:
        peers, length = (lax.axis_size(axis), array.shape[dim])
        up = [(i, (i + 1) % peers) for i in range(peers - 1)]
        down = [(j, i) for i, j in up]
        last = lax.slice_in_dim(array, length - width, length, axis=dim)
        initial = lax.slice_in_dim(array, 0, width, axis=dim)
        before = lax.ppermute(last, axis, up)
        after = lax.ppermute(initial, axis, down)
        array = jnp.concatenate([before, array, after], axis=dim)
    return array


def masked_softmax(scores, allowed):
    masked = jnp.where(allowed, scores, -jnp.inf)
    row_peak = jnp.max(masked, axis=-1, keepdims=True)
    expon_terms = jnp.where(allowed, jnp.exp(masked - row_peak), 0.0)
    return expon_terms / jnp.sum(expon_terms, axis=-1, keepdims=True)


def share_block(stacked, root_index):
    return broadcast(stacked, "seq", root_index)


def local_by_rows(query_rows, key_rows, value_rows, rand_blocks, out_weight):
    tokens, features = query_rows.shape
    head_width = HD
    head_count = features // head_width
    blocks = tokens // BLK
    seq_count = lax.axis_size("seq")
    seq_index = lax.axis_index("seq")
    head_index = lax.axis_index("head")
    block_total = blocks * seq_count
    score_scale = 1.0 / math.sqrt(head_width)
    request_count = blocks * head_count * R
    slot_depth = (request_count + seq_count - 1) // seq_count
    first_rows = jnp.stack((query_rows, key_rows, value_rows))
    final_rows = jnp.stack((query_rows, key_rows, value_rows))
    first_glob = share_block(first_rows, 0)
    final_glob = share_block(final_rows, seq_count - 1)
    paired = jnp.stack((key_rows, value_rows))
    extended = padded(paired, (("seq", 1),), BLK)
    ext_heads = extended.reshape(2, blocks + 2, BLK, head_count, head_width).transpose(
        0, 3, 1, 2, 4
    )
    group_table = lax.dynamic_slice_in_dim(rand_blocks, head_index * head_count, head_count, 1)
    all_requests = group_table.reshape(seq_count, request_count)
    all_owner = all_requests // blocks
    request_order = jnp.arange(request_count, dtype=jnp.int32)
    earlier_request = request_order[None, :] < request_order[:, None]
    same_owner = all_owner[:, :, None] == all_owner[:, None, :]
    all_position = jnp.sum(same_owner & earlier_request[None], axis=2)
    owned_here = all_owner == seq_index
    slot_range = jnp.arange(slot_depth, dtype=jnp.int32)
    picked = owned_here[:, None, :] & (all_position[:, None, :] == slot_range[None, :, None])
    picked_request = jnp.sum(jnp.where(picked, request_order[None, None, :], 0), axis=2)
    picked_block = jnp.take_along_axis(all_requests, picked_request, axis=1) - seq_index * blocks
    picked_block = jnp.clip(picked_block, 0, blocks - 1).reshape(-1)
    picked_head = (picked_request // R % head_count).reshape(-1)
    local_pairs = paired.reshape(2, blocks, BLK, head_count, head_width)
    outgoing = local_pairs[:, picked_block, :, picked_head, :]
    outgoing = outgoing.reshape(seq_count, slot_depth, 2, BLK, head_width)
    received = lax.all_to_all(outgoing, "seq", split_axis=0, concat_axis=0, tiled=True)
    my_requests = lax.dynamic_slice_in_dim(all_requests, seq_index, 1, 0)[0]
    my_position = lax.dynamic_slice_in_dim(all_position, seq_index, 1, 0)[0]
    my_owner = my_requests // blocks
    rand_pairs = jnp.take(
        received.reshape(seq_count * slot_depth, 2, BLK, head_width),
        my_owner * slot_depth + my_position,
        axis=0,
    )
    rand_pairs = rand_pairs.reshape(blocks, head_count, R, 2, BLK, head_width).transpose(
        3, 1, 0, 2, 4, 5
    )
    block_ids = seq_index * blocks + jnp.arange(blocks, dtype=jnp.int32)
    base_slots = jnp.stack(
        [
            jnp.zeros((blocks,), jnp.int32),
            jnp.full((blocks,), block_total - 1, jnp.int32),
            jnp.clip(block_ids - 1, 0, block_total - 1),
            block_ids,
            jnp.clip(block_ids + 1, 0, block_total - 1),
        ],
        axis=1,
    )
    my_table = my_requests.reshape(blocks, head_count, R).transpose(1, 0, 2)
    slot_ids = jnp.concatenate(
        [jnp.broadcast_to(base_slots[None], (head_count, blocks, 5)), my_table], axis=2
    )
    slot_count = slot_ids.shape[2]
    equal_pair = slot_ids[:, :, :, None] == slot_ids[:, :, None, :]
    earlier = jnp.arange(slot_count)[None, :] < jnp.arange(slot_count)[:, None]
    slot_live = jnp.logical_not(jnp.any(equal_pair & earlier[None, None], axis=3))
    key_live = jnp.repeat(slot_live, BLK, axis=2)
    window_index = jnp.arange(blocks)[:, None] + jnp.arange(3)[None, :]
    query_heads = query_rows.reshape(blocks, BLK, head_count, head_width).transpose(2, 0, 1, 3)
    first_heads = first_glob.reshape(3, BLK, head_count, head_width).transpose(0, 2, 1, 3)
    final_heads = final_glob.reshape(3, BLK, head_count, head_width).transpose(0, 2, 1, 3)
    target_heads = max(1, 512 // (blocks * BLK))
    heads_step = max(
        (
            width
            for width in range(1, head_count + 1)
            if head_count % width == 0 and width <= target_heads
        )
    )

    def collect(ext_part, first_block, final_block, rand_part):
        steps_here = ext_part.shape[0]
        window_blocks = ext_part[:, window_index]
        glob_blocks = jnp.stack((first_block, final_block), axis=1)[:, None]
        joined = jnp.concatenate([glob_blocks, window_blocks, rand_part], axis=2)
        return joined.reshape(steps_here, blocks, slot_count * BLK, head_width)

    def attend(head_items):
        (
            query_one,
            key_ext,
            value_ext,
            key_first,
            value_first,
            key_final,
            value_final,
            key_rand,
            value_rand,
            live_one,
        ) = head_items
        keys_sel = collect(key_ext, key_first, key_final, key_rand)
        values_sel = collect(value_ext, value_first, value_final, value_rand)
        scores = (
            jnp.einsum("hibd,hikd->hibk", query_one, keys_sel, preferred_element_type=jnp.float32)
            * score_scale
        )
        weights = masked_softmax(scores, live_one[:, :, None, :]).astype(jnp.bfloat16)
        mixed = jnp.einsum(
            "hibk,hikd->hibd", weights, values_sel, preferred_element_type=jnp.float32
        )
        return mixed.astype(jnp.bfloat16)

    def split_heads(array):
        return array.reshape((head_count // heads_step, heads_step) + array.shape[1:])

    head_inputs = (
        query_heads,
        ext_heads[0],
        ext_heads[1],
        first_heads[1],
        first_heads[2],
        final_heads[1],
        final_heads[2],
        rand_pairs[0],
        rand_pairs[1],
        key_live,
    )
    block_heads = lax.map(attend, tuple((split_heads(item) for item in head_inputs)))
    block_heads = block_heads.reshape(head_count, blocks, BLK, head_width)
    attended = block_heads.transpose(1, 2, 0, 3).reshape(tokens, features)
    glob_query = jnp.concatenate((first_glob[0], final_glob[0]), axis=0).reshape(
        2 * BLK, head_count, head_width
    )
    key_heads = key_rows.reshape(tokens, head_count, head_width)
    value_wide = value_rows.reshape(tokens, head_count, head_width).astype(jnp.float32)
    glob_scores = (
        jnp.einsum("rhd,thd->hrt", glob_query, key_heads, preferred_element_type=jnp.float32)
        * score_scale
    )
    local_peak = jnp.max(glob_scores, axis=2)
    row_peak = lax.pmax(local_peak, "seq")
    expon_terms = jnp.exp(glob_scores - row_peak[:, :, None])
    denoms = jnp.sum(expon_terms, axis=2)
    numer_terms = jnp.einsum(
        "hrt,thd->hrd", expon_terms, value_wide, preferred_element_type=jnp.float32
    )
    numer_terms, denoms = lax.psum((numer_terms, denoms), "seq")
    glob_out = (
        (numer_terms / denoms[:, :, None])
        .astype(jnp.bfloat16)
        .transpose(1, 0, 2)
        .reshape(2 * BLK, features)
    )
    head_block = jnp.where(seq_index == 0, glob_out[:BLK], attended)
    attended = attended.at[:BLK].set(head_block)
    tail_block = jnp.where(seq_index == seq_count - 1, glob_out[BLK:], attended)
    attended = attended.at[tokens - BLK :].set(tail_block)
    partial_terms = lax.dot_general(
        lax.all_gather(out_weight, "seq", axis=0, tiled=True),
        attended,
        (((1,), (1,)), ((), ())),
        preferred_element_type=jnp.float32,
    )
    summed = lax.psum_scatter(
        partial_terms.astype(jnp.bfloat16), "head", scatter_dimension=0, tiled=True
    ).astype(jnp.float32)
    return summed.T.astype(jnp.bfloat16)


def spread_kernel(query_ref, key_ref, value_ref, out_ref):
    peers, heads, _, _, width = out_ref.shape
    for which, ref in enumerate((query_ref, key_ref, value_ref)):
        for peer in range(peers):
            for head in range(heads):
                start = (peer * heads + head) * width
                out_ref[peer, head, which] = ref[:, start : start + width]


def spread(query_rows, key_rows, value_rows, peers):
    tokens, features = query_rows.shape
    heads = features // HD // peers
    return pl.pallas_call(
        spread_kernel,
        out_shape=jax.ShapeDtypeStruct((peers, heads, 3, tokens, HD), query_rows.dtype),
        cost_estimate=pl.CostEstimate(
            flops=0, bytes_accessed=12 * tokens * features, transcendentals=0
        ),
    )(query_rows, key_rows, value_rows)


def attend_kernel(head, rows_ref, bias_ref, out_ref):
    groups = rows_ref.shape[0]
    tokens = rows_ref.shape[3]
    factor = math.log2(math.e) / math.sqrt(HD)
    keys = jnp.concatenate([rows_ref[group, head, 1] for group in range(groups)], axis=0)
    values = jnp.concatenate([rows_ref[group, head, 2] for group in range(groups)], axis=0)
    for group in range(groups):
        scores = lax.dot_general(
            rows_ref[group, head, 0],
            keys,
            (((1,), (1,)), ((), ())),
            preferred_element_type=jnp.float32,
        )
        scores = scores * factor + bias_ref[head, group : group + 1, :]
        peak = jnp.max(scores, axis=1, keepdims=True)
        terms = jnp.exp2(scores - peak)
        denom = jnp.sum(terms, axis=1, keepdims=True)
        mixed = jnp.dot(
            terms.astype(jnp.bfloat16), values, preferred_element_type=jnp.float32
        )
        out_ref[group * tokens : (group + 1) * tokens, :] = (mixed / denom).astype(out_ref.dtype)


def attend_head(rows, bias, head):
    groups, _, _, tokens, _ = rows.shape
    total = groups * tokens
    return pl.pallas_call(
        functools.partial(attend_kernel, head),
        in_specs=[ARRAY] * 2,
        out_shape=jax.ShapeDtypeStruct((total, HD), rows.dtype),
        compiler_params=pltpu.CompilerParams(vmem_limit_bytes=VMEM),
        cost_estimate=pl.CostEstimate(
            flops=4 * total * total * HD,
            bytes_accessed=8 * total * HD,
            transcendentals=total * total,
        ),
    )(rows, bias)


def product_tile(owner_ref, pieces, weight_ref, tile):
    heads = len(pieces) // owner_ref.shape[0]
    width = heads * HD
    rows = jnp.concatenate([piece[tile, :] for piece in pieces], axis=1)
    columns = [
        weight_ref[:, pl.ds(pl.multiple_of(owner_ref[k] * width, width), width)]
        for k in range(owner_ref.shape[0])
    ]
    return lax.dot_general(
        rows,
        jnp.concatenate(columns, axis=1),
        (((1,), (1,)), ((), ())),
        preferred_element_type=jnp.float32,
    )


def early_kernel(owner_ref, weight_ref, *refs):
    *pieces, total_ref = refs
    for start in range(0, total_ref.shape[0], TILE):
        tile = slice(start, start + TILE)
        total_ref[tile, :] = product_tile(owner_ref, pieces, weight_ref, tile)


def late_kernel(owner_ref, side_ref, weight_ref, total_ref, *refs):
    *pieces, send_ref, keep_ref = refs
    half = send_ref.shape[1]
    for start in range(0, total_ref.shape[0], TILE):
        tile = slice(start, start + TILE)
        summed = total_ref[tile, :] + product_tile(owner_ref, pieces, weight_ref, tile)
        low = summed[:, :half].astype(send_ref.dtype)
        high = summed[:, half:].astype(send_ref.dtype)
        first = side_ref[0] == 0
        send_ref[tile, :] = jnp.where(first, high, low)
        keep_ref[tile, :] = jnp.where(first, low, high)


def project_early(owners, pieces, weight):
    total, width = pieces[0].shape
    outs = weight.shape[0]
    return pl.pallas_call(
        early_kernel,
        in_specs=[SCALARS] + [ARRAY] * (1 + len(pieces)),
        out_shape=jax.ShapeDtypeStruct((total, outs), jnp.float32),
        compiler_params=pltpu.CompilerParams(vmem_limit_bytes=VMEM),
        cost_estimate=pl.CostEstimate(
            flops=2 * total * outs * width * len(pieces),
            bytes_accessed=2 * len(pieces) * width * (total + outs) + 4 * total * outs,
            transcendentals=0,
        ),
    )(owners, weight, *pieces)


def project_late(owners, side, pieces, weight, so_far):
    total, width = pieces[0].shape
    outs = weight.shape[0]
    return pl.pallas_call(
        late_kernel,
        in_specs=[SCALARS] * 2 + [ARRAY] * (2 + len(pieces)),
        out_shape=[jax.ShapeDtypeStruct((total, outs // 2), pieces[0].dtype)] * 2,
        compiler_params=pltpu.CompilerParams(vmem_limit_bytes=VMEM),
        cost_estimate=pl.CostEstimate(
            flops=2 * total * outs * width * len(pieces),
            bytes_accessed=2 * len(pieces) * width * (total + outs) + 6 * total * outs,
            transcendentals=0,
        ),
    )(owners, side, weight, so_far, *pieces)


def add_kernel(row_ref, keep_ref, other_ref, *out_refs):
    tokens = out_refs[0].shape[0]
    for apart, out_ref in enumerate(out_refs):
        rows = pl.ds(pl.multiple_of((row_ref[0] ^ apart) * tokens, tokens), tokens)
        out_ref[...] = (
            keep_ref[rows, :].astype(jnp.float32) + other_ref[rows, :].astype(jnp.float32)
        ).astype(out_ref.dtype)


def add_and_part(row, keep, other, parts):
    total, width = keep.shape
    return pl.pallas_call(
        add_kernel,
        in_specs=[SCALARS] + [ARRAY] * 2,
        out_shape=[jax.ShapeDtypeStruct((total // parts, width), keep.dtype)] * parts,
        compiler_params=pltpu.CompilerParams(vmem_limit_bytes=VMEM),
        cost_estimate=pl.CostEstimate(
            flops=total * width, bytes_accessed=6 * total * width, transcendentals=0
        ),
    )(row[None], keep, other)


def assemble_kernel(seq_ref, head_ref, near_ref, crossed_ref, *refs):
    *arrived, out_ref = refs
    reach = len(arrived) // 2
    width = arrived[0].shape[1]
    near = near_ref[0] == 1
    for i in range(reach):
        spot = 2 * ((seq_ref[0] % reach) ^ i)
        mine = pl.ds(pl.multiple_of((spot + head_ref[0]) * width, width), width)
        theirs = pl.ds(pl.multiple_of((spot + 1 - head_ref[0]) * width, width), width)
        out_ref[:, mine] = jnp.where(near, arrived[i][...], arrived[i + reach][...])
        out_ref[:, theirs] = crossed_ref[i]


def assemble(seq_index, head_index, near, crossed, arrived):
    tokens, width = arrived[0].shape
    return pl.pallas_call(
        assemble_kernel,
        in_specs=[SCALARS] * 3 + [ARRAY] * (1 + len(arrived)),
        out_shape=jax.ShapeDtypeStruct((tokens, width * len(arrived)), crossed.dtype),
        compiler_params=pltpu.CompilerParams(vmem_limit_bytes=VMEM),
    )(seq_index[None], head_index[None], near[None], crossed, *arrived)


def key_bias(rand_blocks, head_start, heads):
    block_total = rand_blocks.shape[0]
    ids = jnp.arange(block_total, dtype=jnp.int32)
    near = jnp.abs(ids[:, None] - ids[None, :]) <= 1
    ends = (ids == 0) | (ids == block_total - 1)
    fixed = near | ends[None, :] | ends[:, None]
    chosen = lax.dynamic_slice_in_dim(rand_blocks, head_start, heads, 1)
    named = jnp.any(chosen[:, :, :, None] == ids, axis=2).transpose(1, 0, 2)
    live = named | fixed[None]
    return jnp.repeat(jnp.where(live, 0.0, -1e30).astype(jnp.float32), BLK, axis=2)


def ring_order(peers):
    return list(range(0, peers, 2)) + list(range(peers - 1, 0, -2))


def local_by_heads(query_rows, key_rows, value_rows, rand_blocks, out_weight):
    tokens, features = query_rows.shape
    peers = lax.axis_size("seq")
    seq_index = lax.axis_index("seq")
    head_index = lax.axis_index("head")
    heads = features // HD // peers
    order = ring_order(peers)
    onward = [(order[i], order[(i + 1) % peers]) for i in range(peers)]
    back = [(target, source) for source, target in onward]
    outgoing = spread(query_rows, key_rows, value_rows, peers)
    bias = key_bias(rand_blocks, head_index * (features // HD) + seq_index * heads, heads)
    reach = peers // 2
    far = {}
    rows = lax.all_to_all(outgoing, "seq", split_axis=0, concat_axis=0, tiled=True)
    for head in range(heads):
        mine = attend_head(rows, bias, head)
        ahead, behind = (mine, mine)
        far[head, 0] = mine
        for step in range(1, reach):
            ahead = lax.ppermute(ahead, "seq", onward)
            behind = lax.ppermute(behind, "seq", back)
            far[head, step] = ahead
            far[head, -step] = behind
        if head % 2 == 0:
            far[head, reach] = lax.ppermute(ahead, "seq", onward)
        else:
            far[head, reach] = lax.ppermute(behind, "seq", back)
    place = jnp.where(seq_index % 2 == 0, seq_index // 2, peers - (seq_index + 1) // 2)

    def gather_args(steps):
        spots = (place - jnp.array(steps, jnp.int32)) % peers
        owners = jnp.where(spots < reach, 2 * spots, 2 * (peers - spots) - 1)
        return owners, [far[head, step] for step in steps for head in range(heads)]

    steps = [0] + [step for hop in range(1, reach) for step in (hop, -hop)] + [reach]
    owners, pieces = gather_args(steps[:EARLY])
    so_far = project_early(owners, pieces, out_weight)
    owners, pieces = gather_args(steps[EARLY:])
    send, keep = project_late(owners, head_index[None], pieces, out_weight, so_far)
    swap = [(0, 1), (1, 0)]
    parts = add_and_part(seq_index, keep, lax.ppermute(send, "head", swap), peers)
    arrived = {0: parts[0]}
    for apart in SEND_ORDER:
        pairs = [(i, i ^ apart) for i in range(peers)]
        arrived[apart] = lax.ppermute(parts[apart], "seq", pairs)
    near = (seq_index // reach == head_index).astype(jnp.int32)
    theirs = [jnp.where(near == 1, arrived[i + reach], arrived[i]) for i in range(reach)]
    crossed = lax.ppermute(jnp.stack(theirs), "head", swap)
    return assemble(seq_index, head_index, near, crossed, [arrived[i] for i in range(peers)])


def local(query_rows, key_rows, value_rows, rand_blocks, out_weight):
    tokens, features = query_rows.shape
    peers = lax.axis_size("seq")
    even = features // HD % peers == 0
    if tokens == BLK and peers == 8 and lax.axis_size("head") == 2 and even:
        return local_by_heads(query_rows, key_rows, value_rows, rand_blocks, out_weight)
    return local_by_rows(query_rows, key_rows, value_rows, rand_blocks, out_weight)


def solution(mesh):
    placed = (
        P(("rep", "seq"), "head"),
        P(("rep", "seq"), "head"),
        P(("rep", "seq"), "head"),
        P("rep", None, None),
        P("seq", "head"),
    )
    return jax.shard_map(
        local, mesh=mesh, in_specs=placed, out_specs=P(("rep", "seq"), "head"), check_vma=False
    )
```

```python
import functools
import math

import jax
import jax.numpy as jnp
from jax import lax
from jax.experimental import pallas as pl
from jax.experimental.pallas import tpu as pltpu
from jax.sharding import PartitionSpec as P

HD = 128
BLK = 128
R = 3
VMEM = 20 << 20
TILE = 256
EARLY = 6
PEERS = 8
EARLY_STEPS = 0
ROWS_ORDER = (4, 6, 2, 3, 1, 5, 7)
SEND_ORDER = (4, 6, 5, 7, 2, 3, 1)
SCALARS = pl.BlockSpec(memory_space=pltpu.SMEM)
ARRAY = pl.BlockSpec(memory_space=pltpu.VMEM)


def broadcast(block, axis, owner):
    block = jnp.where(lax.axis_index(axis) == owner, block, jnp.zeros_like(block))
    return lax.psum(block, axis)


def padded(array, sides, width):
    for axis, dim in sides:
        peers, length = (lax.axis_size(axis), array.shape[dim])
        up = [(i, (i + 1) % peers) for i in range(peers - 1)]
        down = [(j, i) for i, j in up]
        last = lax.slice_in_dim(array, length - width, length, axis=dim)
        initial = lax.slice_in_dim(array, 0, width, axis=dim)
        before = lax.ppermute(last, axis, up)
        after = lax.ppermute(initial, axis, down)
        array = jnp.concatenate([before, array, after], axis=dim)
    return array


def masked_softmax(scores, allowed):
    masked = jnp.where(allowed, scores, -jnp.inf)
    row_peak = jnp.max(masked, axis=-1, keepdims=True)
    expon_terms = jnp.where(allowed, jnp.exp(masked - row_peak), 0.0)
    return expon_terms / jnp.sum(expon_terms, axis=-1, keepdims=True)


def share_block(stacked, root_index):
    return broadcast(stacked, "seq", root_index)


def local_by_rows(query_rows, key_rows, value_rows, rand_blocks, out_weight):
    tokens, features = query_rows.shape
    head_width = HD
    head_count = features // head_width
    blocks = tokens // BLK
    seq_count = lax.axis_size("seq")
    seq_index = lax.axis_index("seq")
    head_index = lax.axis_index("head")
    block_total = blocks * seq_count
    score_scale = 1.0 / math.sqrt(head_width)
    request_count = blocks * head_count * R
    slot_depth = (request_count + seq_count - 1) // seq_count
    first_rows = jnp.stack((query_rows, key_rows, value_rows))
    final_rows = jnp.stack((query_rows, key_rows, value_rows))
    first_glob = share_block(first_rows, 0)
    final_glob = share_block(final_rows, seq_count - 1)
    paired = jnp.stack((key_rows, value_rows))
    extended = padded(paired, (("seq", 1),), BLK)
    ext_heads = extended.reshape(2, blocks + 2, BLK, head_count, head_width).transpose(
        0, 3, 1, 2, 4
    )
    group_table = lax.dynamic_slice_in_dim(rand_blocks, head_index * head_count, head_count, 1)
    all_requests = group_table.reshape(seq_count, request_count)
    all_owner = all_requests // blocks
    request_order = jnp.arange(request_count, dtype=jnp.int32)
    earlier_request = request_order[None, :] < request_order[:, None]
    same_owner = all_owner[:, :, None] == all_owner[:, None, :]
    all_position = jnp.sum(same_owner & earlier_request[None], axis=2)
    owned_here = all_owner == seq_index
    slot_range = jnp.arange(slot_depth, dtype=jnp.int32)
    picked = owned_here[:, None, :] & (all_position[:, None, :] == slot_range[None, :, None])
    picked_request = jnp.sum(jnp.where(picked, request_order[None, None, :], 0), axis=2)
    picked_block = jnp.take_along_axis(all_requests, picked_request, axis=1) - seq_index * blocks
    picked_block = jnp.clip(picked_block, 0, blocks - 1).reshape(-1)
    picked_head = (picked_request // R % head_count).reshape(-1)
    local_pairs = paired.reshape(2, blocks, BLK, head_count, head_width)
    outgoing = local_pairs[:, picked_block, :, picked_head, :]
    outgoing = outgoing.reshape(seq_count, slot_depth, 2, BLK, head_width)
    received = lax.all_to_all(outgoing, "seq", split_axis=0, concat_axis=0, tiled=True)
    my_requests = lax.dynamic_slice_in_dim(all_requests, seq_index, 1, 0)[0]
    my_position = lax.dynamic_slice_in_dim(all_position, seq_index, 1, 0)[0]
    my_owner = my_requests // blocks
    rand_pairs = jnp.take(
        received.reshape(seq_count * slot_depth, 2, BLK, head_width),
        my_owner * slot_depth + my_position,
        axis=0,
    )
    rand_pairs = rand_pairs.reshape(blocks, head_count, R, 2, BLK, head_width).transpose(
        3, 1, 0, 2, 4, 5
    )
    block_ids = seq_index * blocks + jnp.arange(blocks, dtype=jnp.int32)
    base_slots = jnp.stack(
        [
            jnp.zeros((blocks,), jnp.int32),
            jnp.full((blocks,), block_total - 1, jnp.int32),
            jnp.clip(block_ids - 1, 0, block_total - 1),
            block_ids,
            jnp.clip(block_ids + 1, 0, block_total - 1),
        ],
        axis=1,
    )
    my_table = my_requests.reshape(blocks, head_count, R).transpose(1, 0, 2)
    slot_ids = jnp.concatenate(
        [jnp.broadcast_to(base_slots[None], (head_count, blocks, 5)), my_table], axis=2
    )
    slot_count = slot_ids.shape[2]
    equal_pair = slot_ids[:, :, :, None] == slot_ids[:, :, None, :]
    earlier = jnp.arange(slot_count)[None, :] < jnp.arange(slot_count)[:, None]
    slot_live = jnp.logical_not(jnp.any(equal_pair & earlier[None, None], axis=3))
    key_live = jnp.repeat(slot_live, BLK, axis=2)
    window_index = jnp.arange(blocks)[:, None] + jnp.arange(3)[None, :]
    query_heads = query_rows.reshape(blocks, BLK, head_count, head_width).transpose(2, 0, 1, 3)
    first_heads = first_glob.reshape(3, BLK, head_count, head_width).transpose(0, 2, 1, 3)
    final_heads = final_glob.reshape(3, BLK, head_count, head_width).transpose(0, 2, 1, 3)
    target_heads = max(1, 512 // (blocks * BLK))
    heads_step = max(
        (
            width
            for width in range(1, head_count + 1)
            if head_count % width == 0 and width <= target_heads
        )
    )

    def collect(ext_part, first_block, final_block, rand_part):
        steps_here = ext_part.shape[0]
        window_blocks = ext_part[:, window_index]
        glob_blocks = jnp.stack((first_block, final_block), axis=1)[:, None]
        joined = jnp.concatenate([glob_blocks, window_blocks, rand_part], axis=2)
        return joined.reshape(steps_here, blocks, slot_count * BLK, head_width)

    def attend(head_items):
        (
            query_one,
            key_ext,
            value_ext,
            key_first,
            value_first,
            key_final,
            value_final,
            key_rand,
            value_rand,
            live_one,
        ) = head_items
        keys_sel = collect(key_ext, key_first, key_final, key_rand)
        values_sel = collect(value_ext, value_first, value_final, value_rand)
        scores = (
            jnp.einsum("hibd,hikd->hibk", query_one, keys_sel, preferred_element_type=jnp.float32)
            * score_scale
        )
        weights = masked_softmax(scores, live_one[:, :, None, :]).astype(jnp.bfloat16)
        mixed = jnp.einsum(
            "hibk,hikd->hibd", weights, values_sel, preferred_element_type=jnp.float32
        )
        return mixed.astype(jnp.bfloat16)

    def split_heads(array):
        return array.reshape((head_count // heads_step, heads_step) + array.shape[1:])

    head_inputs = (
        query_heads,
        ext_heads[0],
        ext_heads[1],
        first_heads[1],
        first_heads[2],
        final_heads[1],
        final_heads[2],
        rand_pairs[0],
        rand_pairs[1],
        key_live,
    )
    block_heads = lax.map(attend, tuple((split_heads(item) for item in head_inputs)))
    block_heads = block_heads.reshape(head_count, blocks, BLK, head_width)
    attended = block_heads.transpose(1, 2, 0, 3).reshape(tokens, features)
    glob_query = jnp.concatenate((first_glob[0], final_glob[0]), axis=0).reshape(
        2 * BLK, head_count, head_width
    )
    key_heads = key_rows.reshape(tokens, head_count, head_width)
    value_wide = value_rows.reshape(tokens, head_count, head_width).astype(jnp.float32)
    glob_scores = (
        jnp.einsum("rhd,thd->hrt", glob_query, key_heads, preferred_element_type=jnp.float32)
        * score_scale
    )
    local_peak = jnp.max(glob_scores, axis=2)
    row_peak = lax.pmax(local_peak, "seq")
    expon_terms = jnp.exp(glob_scores - row_peak[:, :, None])
    denoms = jnp.sum(expon_terms, axis=2)
    numer_terms = jnp.einsum(
        "hrt,thd->hrd", expon_terms, value_wide, preferred_element_type=jnp.float32
    )
    numer_terms, denoms = lax.psum((numer_terms, denoms), "seq")
    glob_out = (
        (numer_terms / denoms[:, :, None])
        .astype(jnp.bfloat16)
        .transpose(1, 0, 2)
        .reshape(2 * BLK, features)
    )
    head_block = jnp.where(seq_index == 0, glob_out[:BLK], attended)
    attended = attended.at[:BLK].set(head_block)
    tail_block = jnp.where(seq_index == seq_count - 1, glob_out[BLK:], attended)
    attended = attended.at[tokens - BLK :].set(tail_block)
    partial_terms = lax.dot_general(
        lax.all_gather(out_weight, "seq", axis=0, tiled=True),
        attended,
        (((1,), (1,)), ((), ())),
        preferred_element_type=jnp.float32,
    )
    summed = lax.psum_scatter(
        partial_terms.astype(jnp.bfloat16), "head", scatter_dimension=0, tiled=True
    ).astype(jnp.float32)
    return summed.T.astype(jnp.bfloat16)


def spread_kernel(seq_ref, query_ref, key_ref, value_ref, *out_refs):
    heads = value_ref.shape[1] // HD // PEERS
    for spot, out_ref in enumerate(out_refs):
        head, apart = divmod(spot, PEERS)
        start = ((seq_ref[0] ^ apart) * heads + head) * HD
        lanes = pl.ds(pl.multiple_of(start, HD), HD)
        for which, ref in enumerate((query_ref, key_ref, value_ref)):
            out_ref[which] = ref[:, lanes]


def spread(seq_index, query_rows, key_rows, value_rows):
    tokens, features = query_rows.shape
    heads = features // HD // PEERS
    piece = jax.ShapeDtypeStruct((3, tokens, HD), query_rows.dtype)
    whole = pl.BlockSpec((tokens, features), lambda i: (0, 0))
    return pl.pallas_call(
        spread_kernel,
        grid=(1,),
        in_specs=[SCALARS] + [whole] * 3,
        out_specs=[pl.BlockSpec(piece.shape, lambda i: (0, 0, 0))] * (heads * PEERS),
        out_shape=[piece] * (heads * PEERS),
        cost_estimate=pl.CostEstimate(
            flops=0, bytes_accessed=12 * tokens * features, transcendentals=0
        ),
    )(seq_index[None], query_rows, key_rows, value_rows)


def attend_kernel(head, seq_ref, bias_ref, *refs):
    *pieces, out_ref = refs
    tokens = pieces[0].shape[1]
    factor = math.log2(math.e) / math.sqrt(HD)
    keys = jnp.concatenate([piece[1] for piece in pieces], axis=0)
    values = jnp.concatenate([piece[2] for piece in pieces], axis=0)
    for apart, piece in enumerate(pieces):
        scores = lax.dot_general(
            piece[0], keys, (((1,), (1,)), ((), ())), preferred_element_type=jnp.float32
        )
        scores = scores * factor + bias_ref[head, apart : apart + 1, :]
        peak = jnp.max(scores, axis=1, keepdims=True)
        terms = jnp.exp2(scores - peak)
        denom = jnp.sum(terms, axis=1, keepdims=True)
        mixed = jnp.dot(
            terms.astype(jnp.bfloat16), values, preferred_element_type=jnp.float32
        )
        rows = pl.ds(pl.multiple_of((seq_ref[0] ^ apart) * tokens, tokens), tokens)
        out_ref[rows, :] = (mixed / denom).astype(out_ref.dtype)


def attend_head(seq_index, bias, pieces, head):
    _, tokens, width = pieces[0].shape
    total = len(pieces) * tokens
    return pl.pallas_call(
        functools.partial(attend_kernel, head),
        in_specs=[SCALARS] + [ARRAY] * (1 + len(pieces)),
        out_shape=jax.ShapeDtypeStruct((total, width), pieces[0].dtype),
        compiler_params=pltpu.CompilerParams(vmem_limit_bytes=VMEM),
        cost_estimate=pl.CostEstimate(
            flops=4 * total * total * width,
            bytes_accessed=8 * total * width,
            transcendentals=total * total,
        ),
    )(seq_index[None], bias, *pieces)


def product_tile(owner_ref, pieces, weight_ref, tile):
    heads = len(pieces) // owner_ref.shape[0]
    width = heads * HD
    rows = jnp.concatenate([piece[tile, :] for piece in pieces], axis=1)
    columns = [
        weight_ref[:, pl.ds(pl.multiple_of(owner_ref[k] * width, width), width)]
        for k in range(owner_ref.shape[0])
    ]
    return lax.dot_general(
        rows,
        jnp.concatenate(columns, axis=1),
        (((1,), (1,)), ((), ())),
        preferred_element_type=jnp.float32,
    )


def early_kernel(owner_ref, weight_ref, *refs):
    *pieces, total_ref = refs
    for start in range(0, total_ref.shape[0], TILE):
        tile = slice(start, start + TILE)
        total_ref[tile, :] = product_tile(owner_ref, pieces, weight_ref, tile)


def late_kernel(owner_ref, side_ref, weight_ref, total_ref, *refs):
    *pieces, send_ref, keep_ref = refs
    half = send_ref.shape[1]
    for start in range(0, total_ref.shape[0], TILE):
        tile = slice(start, start + TILE)
        summed = total_ref[tile, :] + product_tile(owner_ref, pieces, weight_ref, tile)
        low = summed[:, :half].astype(send_ref.dtype)
        high = summed[:, half:].astype(send_ref.dtype)
        first = side_ref[0] == 0
        send_ref[tile, :] = jnp.where(first, high, low)
        keep_ref[tile, :] = jnp.where(first, low, high)


def project_early(owners, pieces, weight):
    total, width = pieces[0].shape
    outs = weight.shape[0]
    return pl.pallas_call(
        early_kernel,
        in_specs=[SCALARS] + [ARRAY] * (1 + len(pieces)),
        out_shape=jax.ShapeDtypeStruct((total, outs), jnp.float32),
        compiler_params=pltpu.CompilerParams(vmem_limit_bytes=VMEM),
        cost_estimate=pl.CostEstimate(
            flops=2 * total * outs * width * len(pieces),
            bytes_accessed=2 * len(pieces) * width * (total + outs) + 4 * total * outs,
            transcendentals=0,
        ),
    )(owners, weight, *pieces)


def project_late(owners, side, pieces, weight, so_far):
    total, width = pieces[0].shape
    outs = weight.shape[0]
    return pl.pallas_call(
        late_kernel,
        in_specs=[SCALARS] * 2 + [ARRAY] * (2 + len(pieces)),
        out_shape=[jax.ShapeDtypeStruct((total, outs // 2), pieces[0].dtype)] * 2,
        compiler_params=pltpu.CompilerParams(vmem_limit_bytes=VMEM),
        cost_estimate=pl.CostEstimate(
            flops=2 * total * outs * width * len(pieces),
            bytes_accessed=2 * len(pieces) * width * (total + outs) + 6 * total * outs,
            transcendentals=0,
        ),
    )(owners, side, weight, so_far, *pieces)


def add_kernel(row_ref, keep_ref, other_ref, *out_refs):
    tokens = out_refs[0].shape[0]
    for apart, out_ref in enumerate(out_refs):
        rows = pl.ds(pl.multiple_of((row_ref[0] ^ apart) * tokens, tokens), tokens)
        out_ref[...] = (
            keep_ref[rows, :].astype(jnp.float32) + other_ref[rows, :].astype(jnp.float32)
        ).astype(out_ref.dtype)


def add_and_part(row, keep, other, parts):
    total, width = keep.shape
    return pl.pallas_call(
        add_kernel,
        in_specs=[SCALARS] + [ARRAY] * 2,
        out_shape=[jax.ShapeDtypeStruct((total // parts, width), keep.dtype)] * parts,
        compiler_params=pltpu.CompilerParams(vmem_limit_bytes=VMEM),
        cost_estimate=pl.CostEstimate(
            flops=total * width, bytes_accessed=6 * total * width, transcendentals=0
        ),
    )(row[None], keep, other)


def assemble_kernel(seq_ref, head_ref, near_ref, crossed_ref, *refs):
    *arrived, out_ref = refs
    reach = len(arrived) // 2
    width = arrived[0].shape[1]
    near = near_ref[0] == 1
    for i in range(reach):
        spot = 2 * ((seq_ref[0] % reach) ^ i)
        mine = pl.ds(pl.multiple_of((spot + head_ref[0]) * width, width), width)
        theirs = pl.ds(pl.multiple_of((spot + 1 - head_ref[0]) * width, width), width)
        out_ref[:, mine] = jnp.where(near, arrived[i][...], arrived[i + reach][...])
        out_ref[:, theirs] = crossed_ref[i]


def assemble(seq_index, head_index, near, crossed, arrived):
    tokens, width = arrived[0].shape
    return pl.pallas_call(
        assemble_kernel,
        in_specs=[SCALARS] * 3 + [ARRAY] * (1 + len(arrived)),
        out_shape=jax.ShapeDtypeStruct((tokens, width * len(arrived)), crossed.dtype),
        compiler_params=pltpu.CompilerParams(vmem_limit_bytes=VMEM),
    )(seq_index[None], head_index[None], near[None], crossed, *arrived)


def key_bias(rand_blocks, seq_index, head_start, heads):
    block_total = rand_blocks.shape[0]
    ids = seq_index ^ jnp.arange(block_total, dtype=jnp.int32)
    near = jnp.abs(ids[:, None] - ids[None, :]) <= 1
    ends = (ids == 0) | (ids == block_total - 1)
    fixed = near | ends[None, :] | ends[:, None]
    chosen = lax.dynamic_slice_in_dim(rand_blocks, head_start, heads, 1)[ids]
    named = jnp.any(chosen[:, :, :, None] == ids, axis=2).transpose(1, 0, 2)
    live = named | fixed[None]
    return jnp.repeat(jnp.where(live, 0.0, -1e30).astype(jnp.float32), BLK, axis=2)


def ring_order(peers):
    return list(range(0, peers, 2)) + list(range(peers - 1, 0, -2))


def local_by_heads(query_rows, key_rows, value_rows, rand_blocks, out_weight):
    tokens, features = query_rows.shape
    peers = lax.axis_size("seq")
    seq_index = lax.axis_index("seq")
    head_index = lax.axis_index("head")
    heads = features // HD // peers
    order = ring_order(peers)
    onward = [(order[i], order[(i + 1) % peers]) for i in range(peers)]
    back = [(target, source) for source, target in onward]
    outgoing = spread(seq_index, query_rows, key_rows, value_rows)
    bias = key_bias(rand_blocks, seq_index, head_index * (features // HD) + seq_index * heads, heads)
    reach = peers // 2
    far = {}
    pieces = {}
    for head in range(heads):
        pieces[head, 0] = outgoing[head * peers]
        for apart in ROWS_ORDER:
            pairs = [(i, i ^ apart) for i in range(peers)]
            pieces[head, apart] = lax.ppermute(outgoing[head * peers + apart], "seq", pairs)
    for head in range(heads):
        group = [pieces[head, apart] for apart in range(peers)]
        if head and EARLY_STEPS:
            held = [far[0, 1], far[0, -1]][:EARLY_STEPS]
            *group, = lax.optimization_barrier((*group, *held))[:peers]
        mine = attend_head(seq_index, bias, group, head)
        ahead, behind = (mine, mine)
        far[head, 0] = mine
        for step in range(1, reach):
            ahead = lax.ppermute(ahead, "seq", onward)
            behind = lax.ppermute(behind, "seq", back)
            far[head, step] = ahead
            far[head, -step] = behind
        if head % 2 == 0:
            far[head, reach] = lax.ppermute(ahead, "seq", onward)
        else:
            far[head, reach] = lax.ppermute(behind, "seq", back)
    place = jnp.where(seq_index % 2 == 0, seq_index // 2, peers - (seq_index + 1) // 2)

    def gather_args(steps):
        spots = (place - jnp.array(steps, jnp.int32)) % peers
        owners = jnp.where(spots < reach, 2 * spots, 2 * (peers - spots) - 1)
        return owners, [far[head, step] for step in steps for head in range(heads)]

    steps = [0] + [step for hop in range(1, reach) for step in (hop, -hop)] + [reach]
    owners, pieces = gather_args(steps[:EARLY])
    so_far = project_early(owners, pieces, out_weight)
    owners, pieces = gather_args(steps[EARLY:])
    send, keep = project_late(owners, head_index[None], pieces, out_weight, so_far)
    swap = [(0, 1), (1, 0)]
    parts = add_and_part(seq_index, keep, lax.ppermute(send, "head", swap), peers)
    arrived = {0: parts[0]}
    for apart in SEND_ORDER:
        pairs = [(i, i ^ apart) for i in range(peers)]
        arrived[apart] = lax.ppermute(parts[apart], "seq", pairs)
    near = (seq_index // reach == head_index).astype(jnp.int32)
    theirs = [jnp.where(near == 1, arrived[i + reach], arrived[i]) for i in range(reach)]
    crossed = lax.ppermute(jnp.stack(theirs), "head", swap)
    return assemble(seq_index, head_index, near, crossed, [arrived[i] for i in range(peers)])


def local(query_rows, key_rows, value_rows, rand_blocks, out_weight):
    tokens, features = query_rows.shape
    peers = lax.axis_size("seq")
    even = features // HD % peers == 0
    if tokens == BLK and peers == PEERS and lax.axis_size("head") == 2 and even:
        return local_by_heads(query_rows, key_rows, value_rows, rand_blocks, out_weight)
    return local_by_rows(query_rows, key_rows, value_rows, rand_blocks, out_weight)


def solution(mesh):
    placed = (
        P(("rep", "seq"), "head"),
        P(("rep", "seq"), "head"),
        P(("rep", "seq"), "head"),
        P("rep", None, None),
        P("seq", "head"),
    )
    return jax.shard_map(
        local, mesh=mesh, in_specs=placed, out_specs=P(("rep", "seq"), "head"), check_vma=False
    )
```

```python
import functools
import math

import jax
import jax.numpy as jnp
from jax import lax
from jax.experimental import pallas as pl
from jax.experimental.pallas import tpu as pltpu
from jax.sharding import PartitionSpec as P

HD = 128
BLK = 128
R = 3
VMEM = 20 << 20
TILE = 256
EARLY = 6
PEERS = 8
EARLY_STEPS = 0
HELD = 2
ROWS_ORDER = ((4, 6, 2, 3, 1, 5, 7), (4, 6, 2, 3, 1, 5, 7))
SEND_ORDER = (4, 6, 5, 7, 2, 3, 1)
SCALARS = pl.BlockSpec(memory_space=pltpu.SMEM)
ARRAY = pl.BlockSpec(memory_space=pltpu.VMEM)


def broadcast(block, axis, owner):
    block = jnp.where(lax.axis_index(axis) == owner, block, jnp.zeros_like(block))
    return lax.psum(block, axis)


def padded(array, sides, width):
    for axis, dim in sides:
        peers, length = (lax.axis_size(axis), array.shape[dim])
        up = [(i, (i + 1) % peers) for i in range(peers - 1)]
        down = [(j, i) for i, j in up]
        last = lax.slice_in_dim(array, length - width, length, axis=dim)
        initial = lax.slice_in_dim(array, 0, width, axis=dim)
        before = lax.ppermute(last, axis, up)
        after = lax.ppermute(initial, axis, down)
        array = jnp.concatenate([before, array, after], axis=dim)
    return array


def masked_softmax(scores, allowed):
    masked = jnp.where(allowed, scores, -jnp.inf)
    row_peak = jnp.max(masked, axis=-1, keepdims=True)
    expon_terms = jnp.where(allowed, jnp.exp(masked - row_peak), 0.0)
    return expon_terms / jnp.sum(expon_terms, axis=-1, keepdims=True)


def share_block(stacked, root_index):
    return broadcast(stacked, "seq", root_index)


def local_by_rows(query_rows, key_rows, value_rows, rand_blocks, out_weight):
    tokens, features = query_rows.shape
    head_width = HD
    head_count = features // head_width
    blocks = tokens // BLK
    seq_count = lax.axis_size("seq")
    seq_index = lax.axis_index("seq")
    head_index = lax.axis_index("head")
    block_total = blocks * seq_count
    score_scale = 1.0 / math.sqrt(head_width)
    request_count = blocks * head_count * R
    slot_depth = (request_count + seq_count - 1) // seq_count
    first_rows = jnp.stack((query_rows, key_rows, value_rows))
    final_rows = jnp.stack((query_rows, key_rows, value_rows))
    first_glob = share_block(first_rows, 0)
    final_glob = share_block(final_rows, seq_count - 1)
    paired = jnp.stack((key_rows, value_rows))
    extended = padded(paired, (("seq", 1),), BLK)
    ext_heads = extended.reshape(2, blocks + 2, BLK, head_count, head_width).transpose(
        0, 3, 1, 2, 4
    )
    group_table = lax.dynamic_slice_in_dim(rand_blocks, head_index * head_count, head_count, 1)
    all_requests = group_table.reshape(seq_count, request_count)
    all_owner = all_requests // blocks
    request_order = jnp.arange(request_count, dtype=jnp.int32)
    earlier_request = request_order[None, :] < request_order[:, None]
    same_owner = all_owner[:, :, None] == all_owner[:, None, :]
    all_position = jnp.sum(same_owner & earlier_request[None], axis=2)
    owned_here = all_owner == seq_index
    slot_range = jnp.arange(slot_depth, dtype=jnp.int32)
    picked = owned_here[:, None, :] & (all_position[:, None, :] == slot_range[None, :, None])
    picked_request = jnp.sum(jnp.where(picked, request_order[None, None, :], 0), axis=2)
    picked_block = jnp.take_along_axis(all_requests, picked_request, axis=1) - seq_index * blocks
    picked_block = jnp.clip(picked_block, 0, blocks - 1).reshape(-1)
    picked_head = (picked_request // R % head_count).reshape(-1)
    local_pairs = paired.reshape(2, blocks, BLK, head_count, head_width)
    outgoing = local_pairs[:, picked_block, :, picked_head, :]
    outgoing = outgoing.reshape(seq_count, slot_depth, 2, BLK, head_width)
    received = lax.all_to_all(outgoing, "seq", split_axis=0, concat_axis=0, tiled=True)
    my_requests = lax.dynamic_slice_in_dim(all_requests, seq_index, 1, 0)[0]
    my_position = lax.dynamic_slice_in_dim(all_position, seq_index, 1, 0)[0]
    my_owner = my_requests // blocks
    rand_pairs = jnp.take(
        received.reshape(seq_count * slot_depth, 2, BLK, head_width),
        my_owner * slot_depth + my_position,
        axis=0,
    )
    rand_pairs = rand_pairs.reshape(blocks, head_count, R, 2, BLK, head_width).transpose(
        3, 1, 0, 2, 4, 5
    )
    block_ids = seq_index * blocks + jnp.arange(blocks, dtype=jnp.int32)
    base_slots = jnp.stack(
        [
            jnp.zeros((blocks,), jnp.int32),
            jnp.full((blocks,), block_total - 1, jnp.int32),
            jnp.clip(block_ids - 1, 0, block_total - 1),
            block_ids,
            jnp.clip(block_ids + 1, 0, block_total - 1),
        ],
        axis=1,
    )
    my_table = my_requests.reshape(blocks, head_count, R).transpose(1, 0, 2)
    slot_ids = jnp.concatenate(
        [jnp.broadcast_to(base_slots[None], (head_count, blocks, 5)), my_table], axis=2
    )
    slot_count = slot_ids.shape[2]
    equal_pair = slot_ids[:, :, :, None] == slot_ids[:, :, None, :]
    earlier = jnp.arange(slot_count)[None, :] < jnp.arange(slot_count)[:, None]
    slot_live = jnp.logical_not(jnp.any(equal_pair & earlier[None, None], axis=3))
    key_live = jnp.repeat(slot_live, BLK, axis=2)
    window_index = jnp.arange(blocks)[:, None] + jnp.arange(3)[None, :]
    query_heads = query_rows.reshape(blocks, BLK, head_count, head_width).transpose(2, 0, 1, 3)
    first_heads = first_glob.reshape(3, BLK, head_count, head_width).transpose(0, 2, 1, 3)
    final_heads = final_glob.reshape(3, BLK, head_count, head_width).transpose(0, 2, 1, 3)
    target_heads = max(1, 512 // (blocks * BLK))
    heads_step = max(
        (
            width
            for width in range(1, head_count + 1)
            if head_count % width == 0 and width <= target_heads
        )
    )

    def collect(ext_part, first_block, final_block, rand_part):
        steps_here = ext_part.shape[0]
        window_blocks = ext_part[:, window_index]
        glob_blocks = jnp.stack((first_block, final_block), axis=1)[:, None]
        joined = jnp.concatenate([glob_blocks, window_blocks, rand_part], axis=2)
        return joined.reshape(steps_here, blocks, slot_count * BLK, head_width)

    def attend(head_items):
        (
            query_one,
            key_ext,
            value_ext,
            key_first,
            value_first,
            key_final,
            value_final,
            key_rand,
            value_rand,
            live_one,
        ) = head_items
        keys_sel = collect(key_ext, key_first, key_final, key_rand)
        values_sel = collect(value_ext, value_first, value_final, value_rand)
        scores = (
            jnp.einsum("hibd,hikd->hibk", query_one, keys_sel, preferred_element_type=jnp.float32)
            * score_scale
        )
        weights = masked_softmax(scores, live_one[:, :, None, :]).astype(jnp.bfloat16)
        mixed = jnp.einsum(
            "hibk,hikd->hibd", weights, values_sel, preferred_element_type=jnp.float32
        )
        return mixed.astype(jnp.bfloat16)

    def split_heads(array):
        return array.reshape((head_count // heads_step, heads_step) + array.shape[1:])

    head_inputs = (
        query_heads,
        ext_heads[0],
        ext_heads[1],
        first_heads[1],
        first_heads[2],
        final_heads[1],
        final_heads[2],
        rand_pairs[0],
        rand_pairs[1],
        key_live,
    )
    block_heads = lax.map(attend, tuple((split_heads(item) for item in head_inputs)))
    block_heads = block_heads.reshape(head_count, blocks, BLK, head_width)
    attended = block_heads.transpose(1, 2, 0, 3).reshape(tokens, features)
    glob_query = jnp.concatenate((first_glob[0], final_glob[0]), axis=0).reshape(
        2 * BLK, head_count, head_width
    )
    key_heads = key_rows.reshape(tokens, head_count, head_width)
    value_wide = value_rows.reshape(tokens, head_count, head_width).astype(jnp.float32)
    glob_scores = (
        jnp.einsum("rhd,thd->hrt", glob_query, key_heads, preferred_element_type=jnp.float32)
        * score_scale
    )
    local_peak = jnp.max(glob_scores, axis=2)
    row_peak = lax.pmax(local_peak, "seq")
    expon_terms = jnp.exp(glob_scores - row_peak[:, :, None])
    denoms = jnp.sum(expon_terms, axis=2)
    numer_terms = jnp.einsum(
        "hrt,thd->hrd", expon_terms, value_wide, preferred_element_type=jnp.float32
    )
    numer_terms, denoms = lax.psum((numer_terms, denoms), "seq")
    glob_out = (
        (numer_terms / denoms[:, :, None])
        .astype(jnp.bfloat16)
        .transpose(1, 0, 2)
        .reshape(2 * BLK, features)
    )
    head_block = jnp.where(seq_index == 0, glob_out[:BLK], attended)
    attended = attended.at[:BLK].set(head_block)
    tail_block = jnp.where(seq_index == seq_count - 1, glob_out[BLK:], attended)
    attended = attended.at[tokens - BLK :].set(tail_block)
    partial_terms = lax.dot_general(
        lax.all_gather(out_weight, "seq", axis=0, tiled=True),
        attended,
        (((1,), (1,)), ((), ())),
        preferred_element_type=jnp.float32,
    )
    summed = lax.psum_scatter(
        partial_terms.astype(jnp.bfloat16), "head", scatter_dimension=0, tiled=True
    ).astype(jnp.float32)
    return summed.T.astype(jnp.bfloat16)


def spread_kernel(head, seq_ref, query_ref, key_ref, value_ref, *out_refs):
    heads = value_ref.shape[1] // HD // PEERS
    for apart, out_ref in enumerate(out_refs):
        start = ((seq_ref[0] ^ apart) * heads + head) * HD
        lanes = pl.ds(pl.multiple_of(start, HD), HD)
        for which, ref in enumerate((query_ref, key_ref, value_ref)):
            out_ref[which] = ref[:, lanes]


def spread(seq_index, query_rows, key_rows, value_rows, head):
    tokens, features = query_rows.shape
    piece = jax.ShapeDtypeStruct((3, tokens, HD), query_rows.dtype)
    whole = pl.BlockSpec((tokens, features), lambda i: (0, 0))
    return pl.pallas_call(
        functools.partial(spread_kernel, head),
        grid=(1,),
        in_specs=[SCALARS] + [whole] * 3,
        out_specs=[pl.BlockSpec(piece.shape, lambda i: (0, 0, 0))] * PEERS,
        out_shape=[piece] * PEERS,
        cost_estimate=pl.CostEstimate(
            flops=0, bytes_accessed=12 * tokens * features, transcendentals=0
        ),
    )(seq_index[None], query_rows, key_rows, value_rows)


def attend_kernel(head, seq_ref, bias_ref, *refs):
    *pieces, out_ref = refs
    tokens = pieces[0].shape[1]
    factor = math.log2(math.e) / math.sqrt(HD)
    keys = jnp.concatenate([piece[1] for piece in pieces], axis=0)
    values = jnp.concatenate([piece[2] for piece in pieces], axis=0)
    for apart, piece in enumerate(pieces):
        scores = lax.dot_general(
            piece[0], keys, (((1,), (1,)), ((), ())), preferred_element_type=jnp.float32
        )
        scores = scores * factor + bias_ref[head, apart : apart + 1, :]
        peak = jnp.max(scores, axis=1, keepdims=True)
        terms = jnp.exp2(scores - peak)
        denom = jnp.sum(terms, axis=1, keepdims=True)
        mixed = jnp.dot(
            terms.astype(jnp.bfloat16), values, preferred_element_type=jnp.float32
        )
        rows = pl.ds(pl.multiple_of((seq_ref[0] ^ apart) * tokens, tokens), tokens)
        out_ref[rows, :] = (mixed / denom).astype(out_ref.dtype)


def attend_head(seq_index, bias, pieces, head):
    _, tokens, width = pieces[0].shape
    total = len(pieces) * tokens
    return pl.pallas_call(
        functools.partial(attend_kernel, head),
        in_specs=[SCALARS] + [ARRAY] * (1 + len(pieces)),
        out_shape=jax.ShapeDtypeStruct((total, width), pieces[0].dtype),
        compiler_params=pltpu.CompilerParams(vmem_limit_bytes=VMEM),
        cost_estimate=pl.CostEstimate(
            flops=4 * total * total * width,
            bytes_accessed=8 * total * width,
            transcendentals=total * total,
        ),
    )(seq_index[None], bias, *pieces)


def product_tile(owner_ref, pieces, weight_ref, tile):
    heads = len(pieces) // owner_ref.shape[0]
    width = heads * HD
    rows = jnp.concatenate([piece[tile, :] for piece in pieces], axis=1)
    columns = [
        weight_ref[:, pl.ds(pl.multiple_of(owner_ref[k] * width, width), width)]
        for k in range(owner_ref.shape[0])
    ]
    return lax.dot_general(
        rows,
        jnp.concatenate(columns, axis=1),
        (((1,), (1,)), ((), ())),
        preferred_element_type=jnp.float32,
    )


def early_kernel(owner_ref, weight_ref, *refs):
    *pieces, total_ref = refs
    for start in range(0, total_ref.shape[0], TILE):
        tile = slice(start, start + TILE)
        total_ref[tile, :] = product_tile(owner_ref, pieces, weight_ref, tile)


def late_kernel(owner_ref, side_ref, weight_ref, total_ref, *refs):
    *pieces, send_ref, keep_ref = refs
    half = send_ref.shape[1]
    for start in range(0, total_ref.shape[0], TILE):
        tile = slice(start, start + TILE)
        summed = total_ref[tile, :] + product_tile(owner_ref, pieces, weight_ref, tile)
        low = summed[:, :half].astype(send_ref.dtype)
        high = summed[:, half:].astype(send_ref.dtype)
        first = side_ref[0] == 0
        send_ref[tile, :] = jnp.where(first, high, low)
        keep_ref[tile, :] = jnp.where(first, low, high)


def project_early(owners, pieces, weight):
    total, width = pieces[0].shape
    outs = weight.shape[0]
    return pl.pallas_call(
        early_kernel,
        in_specs=[SCALARS] + [ARRAY] * (1 + len(pieces)),
        out_shape=jax.ShapeDtypeStruct((total, outs), jnp.float32),
        compiler_params=pltpu.CompilerParams(vmem_limit_bytes=VMEM),
        cost_estimate=pl.CostEstimate(
            flops=2 * total * outs * width * len(pieces),
            bytes_accessed=2 * len(pieces) * width * (total + outs) + 4 * total * outs,
            transcendentals=0,
        ),
    )(owners, weight, *pieces)


def project_late(owners, side, pieces, weight, so_far):
    total, width = pieces[0].shape
    outs = weight.shape[0]
    return pl.pallas_call(
        late_kernel,
        in_specs=[SCALARS] * 2 + [ARRAY] * (2 + len(pieces)),
        out_shape=[jax.ShapeDtypeStruct((total, outs // 2), pieces[0].dtype)] * 2,
        compiler_params=pltpu.CompilerParams(vmem_limit_bytes=VMEM),
        cost_estimate=pl.CostEstimate(
            flops=2 * total * outs * width * len(pieces),
            bytes_accessed=2 * len(pieces) * width * (total + outs) + 6 * total * outs,
            transcendentals=0,
        ),
    )(owners, side, weight, so_far, *pieces)


def add_kernel(row_ref, keep_ref, other_ref, *out_refs):
    tokens = out_refs[0].shape[0]
    for apart, out_ref in enumerate(out_refs):
        rows = pl.ds(pl.multiple_of((row_ref[0] ^ apart) * tokens, tokens), tokens)
        out_ref[...] = (
            keep_ref[rows, :].astype(jnp.float32) + other_ref[rows, :].astype(jnp.float32)
        ).astype(out_ref.dtype)


def add_and_part(row, keep, other, parts):
    total, width = keep.shape
    return pl.pallas_call(
        add_kernel,
        in_specs=[SCALARS] + [ARRAY] * 2,
        out_shape=[jax.ShapeDtypeStruct((total // parts, width), keep.dtype)] * parts,
        compiler_params=pltpu.CompilerParams(vmem_limit_bytes=VMEM),
        cost_estimate=pl.CostEstimate(
            flops=total * width, bytes_accessed=6 * total * width, transcendentals=0
        ),
    )(row[None], keep, other)


def assemble_kernel(seq_ref, head_ref, near_ref, crossed_ref, *refs):
    *arrived, out_ref = refs
    reach = len(arrived) // 2
    width = arrived[0].shape[1]
    near = near_ref[0] == 1
    for i in range(reach):
        spot = 2 * ((seq_ref[0] % reach) ^ i)
        mine = pl.ds(pl.multiple_of((spot + head_ref[0]) * width, width), width)
        theirs = pl.ds(pl.multiple_of((spot + 1 - head_ref[0]) * width, width), width)
        out_ref[:, mine] = jnp.where(near, arrived[i][...], arrived[i + reach][...])
        out_ref[:, theirs] = crossed_ref[i]


def assemble(seq_index, head_index, near, crossed, arrived):
    tokens, width = arrived[0].shape
    return pl.pallas_call(
        assemble_kernel,
        in_specs=[SCALARS] * 3 + [ARRAY] * (1 + len(arrived)),
        out_shape=jax.ShapeDtypeStruct((tokens, width * len(arrived)), crossed.dtype),
        compiler_params=pltpu.CompilerParams(vmem_limit_bytes=VMEM),
    )(seq_index[None], head_index[None], near[None], crossed, *arrived)


def key_bias(rand_blocks, seq_index, head_start, heads):
    block_total = rand_blocks.shape[0]
    ids = seq_index ^ jnp.arange(block_total, dtype=jnp.int32)
    near = jnp.abs(ids[:, None] - ids[None, :]) <= 1
    ends = (ids == 0) | (ids == block_total - 1)
    fixed = near | ends[None, :] | ends[:, None]
    chosen = lax.dynamic_slice_in_dim(rand_blocks, head_start, heads, 1)[ids]
    named = jnp.any(chosen[:, :, :, None] == ids, axis=2).transpose(1, 0, 2)
    live = named | fixed[None]
    return jnp.repeat(jnp.where(live, 0.0, -1e30).astype(jnp.float32), BLK, axis=2)


def ring_order(peers):
    return list(range(0, peers, 2)) + list(range(peers - 1, 0, -2))


def local_by_heads(query_rows, key_rows, value_rows, rand_blocks, out_weight):
    tokens, features = query_rows.shape
    peers = lax.axis_size("seq")
    seq_index = lax.axis_index("seq")
    head_index = lax.axis_index("head")
    heads = features // HD // peers
    order = ring_order(peers)
    onward = [(order[i], order[(i + 1) % peers]) for i in range(peers)]
    back = [(target, source) for source, target in onward]
    outgoing = []
    for head in range(heads):
        if head:
            query_rows, _ = lax.optimization_barrier((query_rows, outgoing[0]))
        outgoing += spread(seq_index, query_rows, key_rows, value_rows, head)
    bias = key_bias(rand_blocks, seq_index, head_index * (features // HD) + seq_index * heads, heads)
    reach = peers // 2
    far = {}
    pieces = {}
    for head in range(heads):
        pieces[head, 0] = outgoing[head * peers]
        for spot, apart in enumerate(ROWS_ORDER[head % 2]):
            if head and spot >= len(ROWS_ORDER[0]) - HELD:
                continue
            pairs = [(i, i ^ apart) for i in range(peers)]
            pieces[head, apart] = lax.ppermute(outgoing[head * peers + apart], "seq", pairs)
    for head in range(heads):
        if head:
            for apart in ROWS_ORDER[head % 2][len(ROWS_ORDER[0]) - HELD :]:
                pairs = [(i, i ^ apart) for i in range(peers)]
                piece, _ = lax.optimization_barrier((outgoing[head * peers + apart], far[0, 0]))
                pieces[head, apart] = lax.ppermute(piece, "seq", pairs)
        group = [pieces[head, apart] for apart in range(peers)]
        if head and EARLY_STEPS:
            held = [far[0, 1], far[0, -1]][:EARLY_STEPS]
            *group, = lax.optimization_barrier((*group, *held))[:peers]
        mine = attend_head(seq_index, bias, group, head)
        ahead, behind = (mine, mine)
        far[head, 0] = mine
        for step in range(1, reach):
            ahead = lax.ppermute(ahead, "seq", onward)
            behind = lax.ppermute(behind, "seq", back)
            far[head, step] = ahead
            far[head, -step] = behind
        if head % 2 == 0:
            far[head, reach] = lax.ppermute(ahead, "seq", onward)
        else:
            far[head, reach] = lax.ppermute(behind, "seq", back)
    place = jnp.where(seq_index % 2 == 0, seq_index // 2, peers - (seq_index + 1) // 2)

    def gather_args(steps):
        spots = (place - jnp.array(steps, jnp.int32)) % peers
        owners = jnp.where(spots < reach, 2 * spots, 2 * (peers - spots) - 1)
        return owners, [far[head, step] for step in steps for head in range(heads)]

    steps = [0] + [step for hop in range(1, reach) for step in (hop, -hop)] + [reach]
    owners, pieces = gather_args(steps[:EARLY])
    so_far = project_early(owners, pieces, out_weight)
    owners, pieces = gather_args(steps[EARLY:])
    send, keep = project_late(owners, head_index[None], pieces, out_weight, so_far)
    swap = [(0, 1), (1, 0)]
    parts = add_and_part(seq_index, keep, lax.ppermute(send, "head", swap), peers)
    arrived = {0: parts[0]}
    for apart in SEND_ORDER:
        pairs = [(i, i ^ apart) for i in range(peers)]
        arrived[apart] = lax.ppermute(parts[apart], "seq", pairs)
    near = (seq_index // reach == head_index).astype(jnp.int32)
    theirs = [jnp.where(near == 1, arrived[i + reach], arrived[i]) for i in range(reach)]
    crossed = lax.ppermute(jnp.stack(theirs), "head", swap)
    return assemble(seq_index, head_index, near, crossed, [arrived[i] for i in range(peers)])


def local(query_rows, key_rows, value_rows, rand_blocks, out_weight):
    tokens, features = query_rows.shape
    peers = lax.axis_size("seq")
    even = features // HD % peers == 0
    if tokens == BLK and peers == PEERS and lax.axis_size("head") == 2 and even:
        return local_by_heads(query_rows, key_rows, value_rows, rand_blocks, out_weight)
    return local_by_rows(query_rows, key_rows, value_rows, rand_blocks, out_weight)


def solution(mesh):
    placed = (
        P(("rep", "seq"), "head"),
        P(("rep", "seq"), "head"),
        P(("rep", "seq"), "head"),
        P("rep", None, None),
        P("seq", "head"),
    )
    return jax.shard_map(
        local, mesh=mesh, in_specs=placed, out_specs=P(("rep", "seq"), "head"), check_vma=False
    )
```

```python
import functools
import math

import jax
import jax.numpy as jnp
from jax import lax
from jax.experimental import pallas as pl
from jax.experimental.pallas import tpu as pltpu
from jax.sharding import PartitionSpec as P

HD = 128
BLK = 128
R = 3
VMEM = 20 << 20
TILE = 256
EARLY = 6
PEERS = 8
EARLY_STEPS = 0
HELD = 2
ROWS_ORDER = ((4, 6, 2, 3, 1, 5, 7), (4, 6, 2, 3, 1, 5, 7))
SEND_ORDER = (4, 6, 5, 7, 2, 3, 1)
SCALARS = pl.BlockSpec(memory_space=pltpu.SMEM)
ARRAY = pl.BlockSpec(memory_space=pltpu.VMEM)


def broadcast(block, axis, owner):
    block = jnp.where(lax.axis_index(axis) == owner, block, jnp.zeros_like(block))
    return lax.psum(block, axis)


def padded(array, sides, width):
    for axis, dim in sides:
        peers, length = (lax.axis_size(axis), array.shape[dim])
        up = [(i, (i + 1) % peers) for i in range(peers - 1)]
        down = [(j, i) for i, j in up]
        last = lax.slice_in_dim(array, length - width, length, axis=dim)
        initial = lax.slice_in_dim(array, 0, width, axis=dim)
        before = lax.ppermute(last, axis, up)
        after = lax.ppermute(initial, axis, down)
        array = jnp.concatenate([before, array, after], axis=dim)
    return array


def masked_softmax(scores, allowed):
    masked = jnp.where(allowed, scores, -jnp.inf)
    row_peak = jnp.max(masked, axis=-1, keepdims=True)
    expon_terms = jnp.where(allowed, jnp.exp(masked - row_peak), 0.0)
    return expon_terms / jnp.sum(expon_terms, axis=-1, keepdims=True)


def share_block(stacked, root_index):
    return broadcast(stacked, "seq", root_index)


def local_by_rows(query_rows, key_rows, value_rows, rand_blocks, out_weight):
    tokens, features = query_rows.shape
    head_width = HD
    head_count = features // head_width
    blocks = tokens // BLK
    seq_count = lax.axis_size("seq")
    seq_index = lax.axis_index("seq")
    head_index = lax.axis_index("head")
    block_total = blocks * seq_count
    score_scale = 1.0 / math.sqrt(head_width)
    request_count = blocks * head_count * R
    slot_depth = (request_count + seq_count - 1) // seq_count
    first_rows = jnp.stack((query_rows, key_rows, value_rows))
    final_rows = jnp.stack((query_rows, key_rows, value_rows))
    first_glob = share_block(first_rows, 0)
    final_glob = share_block(final_rows, seq_count - 1)
    paired = jnp.stack((key_rows, value_rows))
    extended = padded(paired, (("seq", 1),), BLK)
    ext_heads = extended.reshape(2, blocks + 2, BLK, head_count, head_width).transpose(
        0, 3, 1, 2, 4
    )
    group_table = lax.dynamic_slice_in_dim(rand_blocks, head_index * head_count, head_count, 1)
    all_requests = group_table.reshape(seq_count, request_count)
    all_owner = all_requests // blocks
    request_order = jnp.arange(request_count, dtype=jnp.int32)
    earlier_request = request_order[None, :] < request_order[:, None]
    same_owner = all_owner[:, :, None] == all_owner[:, None, :]
    all_position = jnp.sum(same_owner & earlier_request[None], axis=2)
    owned_here = all_owner == seq_index
    slot_range = jnp.arange(slot_depth, dtype=jnp.int32)
    picked = owned_here[:, None, :] & (all_position[:, None, :] == slot_range[None, :, None])
    picked_request = jnp.sum(jnp.where(picked, request_order[None, None, :], 0), axis=2)
    picked_block = jnp.take_along_axis(all_requests, picked_request, axis=1) - seq_index * blocks
    picked_block = jnp.clip(picked_block, 0, blocks - 1).reshape(-1)
    picked_head = (picked_request // R % head_count).reshape(-1)
    local_pairs = paired.reshape(2, blocks, BLK, head_count, head_width)
    outgoing = local_pairs[:, picked_block, :, picked_head, :]
    outgoing = outgoing.reshape(seq_count, slot_depth, 2, BLK, head_width)
    received = lax.all_to_all(outgoing, "seq", split_axis=0, concat_axis=0, tiled=True)
    my_requests = lax.dynamic_slice_in_dim(all_requests, seq_index, 1, 0)[0]
    my_position = lax.dynamic_slice_in_dim(all_position, seq_index, 1, 0)[0]
    my_owner = my_requests // blocks
    rand_pairs = jnp.take(
        received.reshape(seq_count * slot_depth, 2, BLK, head_width),
        my_owner * slot_depth + my_position,
        axis=0,
    )
    rand_pairs = rand_pairs.reshape(blocks, head_count, R, 2, BLK, head_width).transpose(
        3, 1, 0, 2, 4, 5
    )
    block_ids = seq_index * blocks + jnp.arange(blocks, dtype=jnp.int32)
    base_slots = jnp.stack(
        [
            jnp.zeros((blocks,), jnp.int32),
            jnp.full((blocks,), block_total - 1, jnp.int32),
            jnp.clip(block_ids - 1, 0, block_total - 1),
            block_ids,
            jnp.clip(block_ids + 1, 0, block_total - 1),
        ],
        axis=1,
    )
    my_table = my_requests.reshape(blocks, head_count, R).transpose(1, 0, 2)
    slot_ids = jnp.concatenate(
        [jnp.broadcast_to(base_slots[None], (head_count, blocks, 5)), my_table], axis=2
    )
    slot_count = slot_ids.shape[2]
    equal_pair = slot_ids[:, :, :, None] == slot_ids[:, :, None, :]
    earlier = jnp.arange(slot_count)[None, :] < jnp.arange(slot_count)[:, None]
    slot_live = jnp.logical_not(jnp.any(equal_pair & earlier[None, None], axis=3))
    key_live = jnp.repeat(slot_live, BLK, axis=2)
    window_index = jnp.arange(blocks)[:, None] + jnp.arange(3)[None, :]
    query_heads = query_rows.reshape(blocks, BLK, head_count, head_width).transpose(2, 0, 1, 3)
    first_heads = first_glob.reshape(3, BLK, head_count, head_width).transpose(0, 2, 1, 3)
    final_heads = final_glob.reshape(3, BLK, head_count, head_width).transpose(0, 2, 1, 3)
    target_heads = max(1, 512 // (blocks * BLK))
    heads_step = max(
        (
            width
            for width in range(1, head_count + 1)
            if head_count % width == 0 and width <= target_heads
        )
    )

    def collect(ext_part, first_block, final_block, rand_part):
        steps_here = ext_part.shape[0]
        window_blocks = ext_part[:, window_index]
        glob_blocks = jnp.stack((first_block, final_block), axis=1)[:, None]
        joined = jnp.concatenate([glob_blocks, window_blocks, rand_part], axis=2)
        return joined.reshape(steps_here, blocks, slot_count * BLK, head_width)

    def attend(head_items):
        (
            query_one,
            key_ext,
            value_ext,
            key_first,
            value_first,
            key_final,
            value_final,
            key_rand,
            value_rand,
            live_one,
        ) = head_items
        keys_sel = collect(key_ext, key_first, key_final, key_rand)
        values_sel = collect(value_ext, value_first, value_final, value_rand)
        scores = (
            jnp.einsum("hibd,hikd->hibk", query_one, keys_sel, preferred_element_type=jnp.float32)
            * score_scale
        )
        weights = masked_softmax(scores, live_one[:, :, None, :]).astype(jnp.bfloat16)
        mixed = jnp.einsum(
            "hibk,hikd->hibd", weights, values_sel, preferred_element_type=jnp.float32
        )
        return mixed.astype(jnp.bfloat16)

    def split_heads(array):
        return array.reshape((head_count // heads_step, heads_step) + array.shape[1:])

    head_inputs = (
        query_heads,
        ext_heads[0],
        ext_heads[1],
        first_heads[1],
        first_heads[2],
        final_heads[1],
        final_heads[2],
        rand_pairs[0],
        rand_pairs[1],
        key_live,
    )
    block_heads = lax.map(attend, tuple((split_heads(item) for item in head_inputs)))
    block_heads = block_heads.reshape(head_count, blocks, BLK, head_width)
    attended = block_heads.transpose(1, 2, 0, 3).reshape(tokens, features)
    glob_query = jnp.concatenate((first_glob[0], final_glob[0]), axis=0).reshape(
        2 * BLK, head_count, head_width
    )
    key_heads = key_rows.reshape(tokens, head_count, head_width)
    value_wide = value_rows.reshape(tokens, head_count, head_width).astype(jnp.float32)
    glob_scores = (
        jnp.einsum("rhd,thd->hrt", glob_query, key_heads, preferred_element_type=jnp.float32)
        * score_scale
    )
    local_peak = jnp.max(glob_scores, axis=2)
    row_peak = lax.pmax(local_peak, "seq")
    expon_terms = jnp.exp(glob_scores - row_peak[:, :, None])
    denoms = jnp.sum(expon_terms, axis=2)
    numer_terms = jnp.einsum(
        "hrt,thd->hrd", expon_terms, value_wide, preferred_element_type=jnp.float32
    )
    numer_terms, denoms = lax.psum((numer_terms, denoms), "seq")
    glob_out = (
        (numer_terms / denoms[:, :, None])
        .astype(jnp.bfloat16)
        .transpose(1, 0, 2)
        .reshape(2 * BLK, features)
    )
    head_block = jnp.where(seq_index == 0, glob_out[:BLK], attended)
    attended = attended.at[:BLK].set(head_block)
    tail_block = jnp.where(seq_index == seq_count - 1, glob_out[BLK:], attended)
    attended = attended.at[tokens - BLK :].set(tail_block)
    partial_terms = lax.dot_general(
        lax.all_gather(out_weight, "seq", axis=0, tiled=True),
        attended,
        (((1,), (1,)), ((), ())),
        preferred_element_type=jnp.float32,
    )
    summed = lax.psum_scatter(
        partial_terms.astype(jnp.bfloat16), "head", scatter_dimension=0, tiled=True
    ).astype(jnp.float32)
    return summed.T.astype(jnp.bfloat16)


def spread_kernel(head, seq_ref, query_ref, key_ref, value_ref, *out_refs):
    heads = value_ref.shape[1] // HD // PEERS
    for apart, out_ref in enumerate(out_refs):
        start = ((seq_ref[0] ^ apart) * heads + head) * HD
        lanes = pl.ds(pl.multiple_of(start, HD), HD)
        for which, ref in enumerate((query_ref, key_ref, value_ref)):
            out_ref[which] = ref[:, lanes]


def spread(seq_index, query_rows, key_rows, value_rows, head):
    tokens, features = query_rows.shape
    piece = jax.ShapeDtypeStruct((3, tokens, HD), query_rows.dtype)
    whole = pl.BlockSpec((tokens, features), lambda i: (0, 0))
    return pl.pallas_call(
        functools.partial(spread_kernel, head),
        grid=(1,),
        in_specs=[SCALARS] + [whole] * 3,
        out_specs=[pl.BlockSpec(piece.shape, lambda i: (0, 0, 0))] * PEERS,
        out_shape=[piece] * PEERS,
        cost_estimate=pl.CostEstimate(
            flops=0, bytes_accessed=12 * tokens * features, transcendentals=0
        ),
    )(seq_index[None], query_rows, key_rows, value_rows)


def attend_kernel(head, seq_ref, bias_ref, *refs):
    *pieces, out_ref = refs
    tokens = pieces[0].shape[1]
    factor = math.log2(math.e) / math.sqrt(HD)
    keys = jnp.concatenate([piece[1] for piece in pieces], axis=0)
    values = jnp.concatenate([piece[2] for piece in pieces], axis=0)
    for apart, piece in enumerate(pieces):
        scores = lax.dot_general(
            piece[0], keys, (((1,), (1,)), ((), ())), preferred_element_type=jnp.float32
        )
        scores = scores * factor + bias_ref[head, apart : apart + 1, :]
        peak = jnp.max(scores, axis=1, keepdims=True)
        terms = jnp.exp2(scores - peak)
        denom = jnp.sum(terms, axis=1, keepdims=True)
        mixed = jnp.dot(
            terms.astype(jnp.bfloat16), values, preferred_element_type=jnp.float32
        )
        rows = pl.ds(pl.multiple_of((seq_ref[0] ^ apart) * tokens, tokens), tokens)
        out_ref[rows, :] = (mixed / denom).astype(out_ref.dtype)


def attend_head(seq_index, bias, pieces, head):
    _, tokens, width = pieces[0].shape
    total = len(pieces) * tokens
    return pl.pallas_call(
        functools.partial(attend_kernel, head),
        in_specs=[SCALARS] + [ARRAY] * (1 + len(pieces)),
        out_shape=jax.ShapeDtypeStruct((total, width), pieces[0].dtype),
        compiler_params=pltpu.CompilerParams(vmem_limit_bytes=VMEM),
        cost_estimate=pl.CostEstimate(
            flops=4 * total * total * width,
            bytes_accessed=8 * total * width,
            transcendentals=total * total,
        ),
    )(seq_index[None], bias, *pieces)


def product_tile(owner_ref, pieces, weight_ref, tile):
    heads = len(pieces) // owner_ref.shape[0]
    width = heads * HD
    rows = jnp.concatenate([piece[tile, :] for piece in pieces], axis=1)
    columns = [
        weight_ref[:, pl.ds(pl.multiple_of(owner_ref[k] * width, width), width)]
        for k in range(owner_ref.shape[0])
    ]
    return lax.dot_general(
        rows,
        jnp.concatenate(columns, axis=1),
        (((1,), (1,)), ((), ())),
        preferred_element_type=jnp.float32,
    )


def early_kernel(owner_ref, weight_ref, *refs):
    *pieces, total_ref = refs
    for start in range(0, total_ref.shape[0], TILE):
        tile = slice(start, start + TILE)
        total_ref[tile, :] = product_tile(owner_ref, pieces, weight_ref, tile)


def late_kernel(owner_ref, side_ref, weight_ref, total_ref, *refs):
    *pieces, out_ref = refs
    half = out_ref.shape[1]
    outs = pl.ds(pl.multiple_of(side_ref[0] * half, half), half)
    for start in range(0, total_ref.shape[0], TILE):
        tile = slice(start, start + TILE)
        product = product_tile(owner_ref, pieces, weight_ref.at[outs, :], tile)
        out_ref[tile, :] = (total_ref[tile, outs] + product).astype(out_ref.dtype)


def project_early(owners, pieces, weight):
    total, width = pieces[0].shape
    outs = weight.shape[0]
    return pl.pallas_call(
        early_kernel,
        in_specs=[SCALARS] + [ARRAY] * (1 + len(pieces)),
        out_shape=jax.ShapeDtypeStruct((total, outs), jnp.float32),
        compiler_params=pltpu.CompilerParams(vmem_limit_bytes=VMEM),
        cost_estimate=pl.CostEstimate(
            flops=2 * total * outs * width * len(pieces),
            bytes_accessed=2 * len(pieces) * width * (total + outs) + 4 * total * outs,
            transcendentals=0,
        ),
    )(owners, weight, *pieces)


def project_late(owners, side, pieces, weight, so_far):
    total, width = pieces[0].shape
    outs = weight.shape[0]
    return pl.pallas_call(
        late_kernel,
        in_specs=[SCALARS] * 2 + [ARRAY] * (2 + len(pieces)),
        out_shape=jax.ShapeDtypeStruct((total, outs // 2), pieces[0].dtype),
        compiler_params=pltpu.CompilerParams(vmem_limit_bytes=VMEM),
        cost_estimate=pl.CostEstimate(
            flops=total * outs * width * len(pieces),
            bytes_accessed=2 * len(pieces) * width * (total + outs) + 6 * total * outs,
            transcendentals=0,
        ),
    )(owners, side, weight, so_far, *pieces)


def add_kernel(row_ref, keep_ref, other_ref, *out_refs):
    tokens = out_refs[0].shape[0]
    for apart, out_ref in enumerate(out_refs):
        rows = pl.ds(pl.multiple_of((row_ref[0] ^ apart) * tokens, tokens), tokens)
        out_ref[...] = (
            keep_ref[rows, :].astype(jnp.float32) + other_ref[rows, :].astype(jnp.float32)
        ).astype(out_ref.dtype)


def add_and_part(row, keep, other, parts):
    total, width = keep.shape
    return pl.pallas_call(
        add_kernel,
        in_specs=[SCALARS] + [ARRAY] * 2,
        out_shape=[jax.ShapeDtypeStruct((total // parts, width), keep.dtype)] * parts,
        compiler_params=pltpu.CompilerParams(vmem_limit_bytes=VMEM),
        cost_estimate=pl.CostEstimate(
            flops=total * width, bytes_accessed=6 * total * width, transcendentals=0
        ),
    )(row[None], keep, other)


def assemble_kernel(seq_ref, head_ref, near_ref, crossed_ref, *refs):
    *arrived, out_ref = refs
    reach = len(arrived) // 2
    width = arrived[0].shape[1]
    near = near_ref[0] == 1
    for i in range(reach):
        spot = 2 * ((seq_ref[0] % reach) ^ i)
        mine = pl.ds(pl.multiple_of((spot + head_ref[0]) * width, width), width)
        theirs = pl.ds(pl.multiple_of((spot + 1 - head_ref[0]) * width, width), width)
        out_ref[:, mine] = jnp.where(near, arrived[i][...], arrived[i + reach][...])
        out_ref[:, theirs] = crossed_ref[i]


def assemble(seq_index, head_index, near, crossed, arrived):
    tokens, width = arrived[0].shape
    return pl.pallas_call(
        assemble_kernel,
        in_specs=[SCALARS] * 3 + [ARRAY] * (1 + len(arrived)),
        out_shape=jax.ShapeDtypeStruct((tokens, width * len(arrived)), crossed.dtype),
        compiler_params=pltpu.CompilerParams(vmem_limit_bytes=VMEM),
    )(seq_index[None], head_index[None], near[None], crossed, *arrived)


def key_bias(rand_blocks, seq_index, head_start, heads):
    block_total = rand_blocks.shape[0]
    ids = seq_index ^ jnp.arange(block_total, dtype=jnp.int32)
    near = jnp.abs(ids[:, None] - ids[None, :]) <= 1
    ends = (ids == 0) | (ids == block_total - 1)
    fixed = near | ends[None, :] | ends[:, None]
    chosen = lax.dynamic_slice_in_dim(rand_blocks, head_start, heads, 1)[ids]
    named = jnp.any(chosen[:, :, :, None] == ids, axis=2).transpose(1, 0, 2)
    live = named | fixed[None]
    return jnp.repeat(jnp.where(live, 0.0, -1e30).astype(jnp.float32), BLK, axis=2)


def ring_order(peers):
    return list(range(0, peers, 2)) + list(range(peers - 1, 0, -2))


def local_by_heads(query_rows, key_rows, value_rows, rand_blocks, out_weight):
    tokens, features = query_rows.shape
    peers = lax.axis_size("seq")
    seq_index = lax.axis_index("seq")
    head_index = lax.axis_index("head")
    heads = features // HD // peers
    order = ring_order(peers)
    onward = [(order[i], order[(i + 1) % peers]) for i in range(peers)]
    back = [(target, source) for source, target in onward]
    outgoing = []
    for head in range(heads):
        if head:
            query_rows, _ = lax.optimization_barrier((query_rows, outgoing[0]))
        outgoing += spread(seq_index, query_rows, key_rows, value_rows, head)
    bias = key_bias(rand_blocks, seq_index, head_index * (features // HD) + seq_index * heads, heads)
    reach = peers // 2
    far = {}
    pieces = {}
    for head in range(heads):
        pieces[head, 0] = outgoing[head * peers]
        for spot, apart in enumerate(ROWS_ORDER[head % 2]):
            if head and spot >= len(ROWS_ORDER[0]) - HELD:
                continue
            pairs = [(i, i ^ apart) for i in range(peers)]
            pieces[head, apart] = lax.ppermute(outgoing[head * peers + apart], "seq", pairs)
    for head in range(heads):
        if head:
            for apart in ROWS_ORDER[head % 2][len(ROWS_ORDER[0]) - HELD :]:
                pairs = [(i, i ^ apart) for i in range(peers)]
                piece, _ = lax.optimization_barrier((outgoing[head * peers + apart], far[0, 0]))
                pieces[head, apart] = lax.ppermute(piece, "seq", pairs)
        group = [pieces[head, apart] for apart in range(peers)]
        if head and EARLY_STEPS:
            held = [far[0, 1], far[0, -1]][:EARLY_STEPS]
            *group, = lax.optimization_barrier((*group, *held))[:peers]
        mine = attend_head(seq_index, bias, group, head)
        ahead, behind = (mine, mine)
        far[head, 0] = mine
        for step in range(1, reach):
            ahead = lax.ppermute(ahead, "seq", onward)
            behind = lax.ppermute(behind, "seq", back)
            far[head, step] = ahead
            far[head, -step] = behind
        if head % 2 == 0:
            far[head, reach] = lax.ppermute(ahead, "seq", onward)
        else:
            far[head, reach] = lax.ppermute(behind, "seq", back)
    place = jnp.where(seq_index % 2 == 0, seq_index // 2, peers - (seq_index + 1) // 2)

    def gather_args(steps):
        spots = (place - jnp.array(steps, jnp.int32)) % peers
        owners = jnp.where(spots < reach, 2 * spots, 2 * (peers - spots) - 1)
        return owners, [far[head, step] for step in steps for head in range(heads)]

    steps = [0] + [step for hop in range(1, reach) for step in (hop, -hop)] + [reach]
    owners, pieces = gather_args(steps[:EARLY])
    so_far = project_early(owners, pieces, out_weight)
    owners, pieces = gather_args(steps[EARLY:])
    send = project_late(owners, 1 - head_index[None], pieces, out_weight, so_far)
    swap = [(0, 1), (1, 0)]
    other = lax.ppermute(send, "head", swap)
    keep = project_late(owners, head_index[None], pieces, out_weight, so_far)
    parts = add_and_part(seq_index, keep, other, peers)
    arrived = {0: parts[0]}
    for apart in SEND_ORDER:
        pairs = [(i, i ^ apart) for i in range(peers)]
        arrived[apart] = lax.ppermute(parts[apart], "seq", pairs)
    near = (seq_index // reach == head_index).astype(jnp.int32)
    theirs = [jnp.where(near == 1, arrived[i + reach], arrived[i]) for i in range(reach)]
    crossed = lax.ppermute(jnp.stack(theirs), "head", swap)
    return assemble(seq_index, head_index, near, crossed, [arrived[i] for i in range(peers)])


def local(query_rows, key_rows, value_rows, rand_blocks, out_weight):
    tokens, features = query_rows.shape
    peers = lax.axis_size("seq")
    even = features // HD % peers == 0
    if tokens == BLK and peers == PEERS and lax.axis_size("head") == 2 and even:
        return local_by_heads(query_rows, key_rows, value_rows, rand_blocks, out_weight)
    return local_by_rows(query_rows, key_rows, value_rows, rand_blocks, out_weight)


def solution(mesh):
    placed = (
        P(("rep", "seq"), "head"),
        P(("rep", "seq"), "head"),
        P(("rep", "seq"), "head"),
        P("rep", None, None),
        P("seq", "head"),
    )
    return jax.shard_map(
        local, mesh=mesh, in_specs=placed, out_specs=P(("rep", "seq"), "head"), check_vma=False
    )
```

```python
import functools
import math

import jax
import jax.numpy as jnp
from jax import lax
from jax.experimental import pallas as pl
from jax.experimental.pallas import tpu as pltpu
from jax.sharding import PartitionSpec as P

HD = 128
BLK = 128
R = 3
VMEM = 20 << 20
TILE = 256
EARLY = 6
PEERS = 8
EARLY_STEPS = 0
HELD = 2
ROWS_ORDER = ((4, 6, 2, 3, 1, 5, 7), (4, 6, 2, 3, 1, 5, 7))
SEND_ORDER = (2, 4, 1, 6, 3, 5, 7)
SCALARS = pl.BlockSpec(memory_space=pltpu.SMEM)
ARRAY = pl.BlockSpec(memory_space=pltpu.VMEM)


def broadcast(block, axis, owner):
    block = jnp.where(lax.axis_index(axis) == owner, block, jnp.zeros_like(block))
    return lax.psum(block, axis)


def padded(array, sides, width):
    for axis, dim in sides:
        peers, length = (lax.axis_size(axis), array.shape[dim])
        up = [(i, (i + 1) % peers) for i in range(peers - 1)]
        down = [(j, i) for i, j in up]
        last = lax.slice_in_dim(array, length - width, length, axis=dim)
        initial = lax.slice_in_dim(array, 0, width, axis=dim)
        before = lax.ppermute(last, axis, up)
        after = lax.ppermute(initial, axis, down)
        array = jnp.concatenate([before, array, after], axis=dim)
    return array


def masked_softmax(scores, allowed):
    masked = jnp.where(allowed, scores, -jnp.inf)
    row_peak = jnp.max(masked, axis=-1, keepdims=True)
    expon_terms = jnp.where(allowed, jnp.exp(masked - row_peak), 0.0)
    return expon_terms / jnp.sum(expon_terms, axis=-1, keepdims=True)


def share_block(stacked, root_index):
    return broadcast(stacked, "seq", root_index)


def local_by_rows(query_rows, key_rows, value_rows, rand_blocks, out_weight):
    tokens, features = query_rows.shape
    head_width = HD
    head_count = features // head_width
    blocks = tokens // BLK
    seq_count = lax.axis_size("seq")
    seq_index = lax.axis_index("seq")
    head_index = lax.axis_index("head")
    block_total = blocks * seq_count
    score_scale = 1.0 / math.sqrt(head_width)
    request_count = blocks * head_count * R
    slot_depth = (request_count + seq_count - 1) // seq_count
    first_rows = jnp.stack((query_rows, key_rows, value_rows))
    final_rows = jnp.stack((query_rows, key_rows, value_rows))
    first_glob = share_block(first_rows, 0)
    final_glob = share_block(final_rows, seq_count - 1)
    paired = jnp.stack((key_rows, value_rows))
    extended = padded(paired, (("seq", 1),), BLK)
    ext_heads = extended.reshape(2, blocks + 2, BLK, head_count, head_width).transpose(
        0, 3, 1, 2, 4
    )
    group_table = lax.dynamic_slice_in_dim(rand_blocks, head_index * head_count, head_count, 1)
    all_requests = group_table.reshape(seq_count, request_count)
    all_owner = all_requests // blocks
    request_order = jnp.arange(request_count, dtype=jnp.int32)
    earlier_request = request_order[None, :] < request_order[:, None]
    same_owner = all_owner[:, :, None] == all_owner[:, None, :]
    all_position = jnp.sum(same_owner & earlier_request[None], axis=2)
    owned_here = all_owner == seq_index
    slot_range = jnp.arange(slot_depth, dtype=jnp.int32)
    picked = owned_here[:, None, :] & (all_position[:, None, :] == slot_range[None, :, None])
    picked_request = jnp.sum(jnp.where(picked, request_order[None, None, :], 0), axis=2)
    picked_block = jnp.take_along_axis(all_requests, picked_request, axis=1) - seq_index * blocks
    picked_block = jnp.clip(picked_block, 0, blocks - 1).reshape(-1)
    picked_head = (picked_request // R % head_count).reshape(-1)
    local_pairs = paired.reshape(2, blocks, BLK, head_count, head_width)
    outgoing = local_pairs[:, picked_block, :, picked_head, :]
    outgoing = outgoing.reshape(seq_count, slot_depth, 2, BLK, head_width)
    received = lax.all_to_all(outgoing, "seq", split_axis=0, concat_axis=0, tiled=True)
    my_requests = lax.dynamic_slice_in_dim(all_requests, seq_index, 1, 0)[0]
    my_position = lax.dynamic_slice_in_dim(all_position, seq_index, 1, 0)[0]
    my_owner = my_requests // blocks
    rand_pairs = jnp.take(
        received.reshape(seq_count * slot_depth, 2, BLK, head_width),
        my_owner * slot_depth + my_position,
        axis=0,
    )
    rand_pairs = rand_pairs.reshape(blocks, head_count, R, 2, BLK, head_width).transpose(
        3, 1, 0, 2, 4, 5
    )
    block_ids = seq_index * blocks + jnp.arange(blocks, dtype=jnp.int32)
    base_slots = jnp.stack(
        [
            jnp.zeros((blocks,), jnp.int32),
            jnp.full((blocks,), block_total - 1, jnp.int32),
            jnp.clip(block_ids - 1, 0, block_total - 1),
            block_ids,
            jnp.clip(block_ids + 1, 0, block_total - 1),
        ],
        axis=1,
    )
    my_table = my_requests.reshape(blocks, head_count, R).transpose(1, 0, 2)
    slot_ids = jnp.concatenate(
        [jnp.broadcast_to(base_slots[None], (head_count, blocks, 5)), my_table], axis=2
    )
    slot_count = slot_ids.shape[2]
    equal_pair = slot_ids[:, :, :, None] == slot_ids[:, :, None, :]
    earlier = jnp.arange(slot_count)[None, :] < jnp.arange(slot_count)[:, None]
    slot_live = jnp.logical_not(jnp.any(equal_pair & earlier[None, None], axis=3))
    key_live = jnp.repeat(slot_live, BLK, axis=2)
    window_index = jnp.arange(blocks)[:, None] + jnp.arange(3)[None, :]
    query_heads = query_rows.reshape(blocks, BLK, head_count, head_width).transpose(2, 0, 1, 3)
    first_heads = first_glob.reshape(3, BLK, head_count, head_width).transpose(0, 2, 1, 3)
    final_heads = final_glob.reshape(3, BLK, head_count, head_width).transpose(0, 2, 1, 3)
    target_heads = max(1, 512 // (blocks * BLK))
    heads_step = max(
        (
            width
            for width in range(1, head_count + 1)
            if head_count % width == 0 and width <= target_heads
        )
    )

    def collect(ext_part, first_block, final_block, rand_part):
        steps_here = ext_part.shape[0]
        window_blocks = ext_part[:, window_index]
        glob_blocks = jnp.stack((first_block, final_block), axis=1)[:, None]
        joined = jnp.concatenate([glob_blocks, window_blocks, rand_part], axis=2)
        return joined.reshape(steps_here, blocks, slot_count * BLK, head_width)

    def attend(head_items):
        (
            query_one,
            key_ext,
            value_ext,
            key_first,
            value_first,
            key_final,
            value_final,
            key_rand,
            value_rand,
            live_one,
        ) = head_items
        keys_sel = collect(key_ext, key_first, key_final, key_rand)
        values_sel = collect(value_ext, value_first, value_final, value_rand)
        scores = (
            jnp.einsum("hibd,hikd->hibk", query_one, keys_sel, preferred_element_type=jnp.float32)
            * score_scale
        )
        weights = masked_softmax(scores, live_one[:, :, None, :]).astype(jnp.bfloat16)
        mixed = jnp.einsum(
            "hibk,hikd->hibd", weights, values_sel, preferred_element_type=jnp.float32
        )
        return mixed.astype(jnp.bfloat16)

    def split_heads(array):
        return array.reshape((head_count // heads_step, heads_step) + array.shape[1:])

    head_inputs = (
        query_heads,
        ext_heads[0],
        ext_heads[1],
        first_heads[1],
        first_heads[2],
        final_heads[1],
        final_heads[2],
        rand_pairs[0],
        rand_pairs[1],
        key_live,
    )
    block_heads = lax.map(attend, tuple((split_heads(item) for item in head_inputs)))
    block_heads = block_heads.reshape(head_count, blocks, BLK, head_width)
    attended = block_heads.transpose(1, 2, 0, 3).reshape(tokens, features)
    glob_query = jnp.concatenate((first_glob[0], final_glob[0]), axis=0).reshape(
        2 * BLK, head_count, head_width
    )
    key_heads = key_rows.reshape(tokens, head_count, head_width)
    value_wide = value_rows.reshape(tokens, head_count, head_width).astype(jnp.float32)
    glob_scores = (
        jnp.einsum("rhd,thd->hrt", glob_query, key_heads, preferred_element_type=jnp.float32)
        * score_scale
    )
    local_peak = jnp.max(glob_scores, axis=2)
    row_peak = lax.pmax(local_peak, "seq")
    expon_terms = jnp.exp(glob_scores - row_peak[:, :, None])
    denoms = jnp.sum(expon_terms, axis=2)
    numer_terms = jnp.einsum(
        "hrt,thd->hrd", expon_terms, value_wide, preferred_element_type=jnp.float32
    )
    numer_terms, denoms = lax.psum((numer_terms, denoms), "seq")
    glob_out = (
        (numer_terms / denoms[:, :, None])
        .astype(jnp.bfloat16)
        .transpose(1, 0, 2)
        .reshape(2 * BLK, features)
    )
    head_block = jnp.where(seq_index == 0, glob_out[:BLK], attended)
    attended = attended.at[:BLK].set(head_block)
    tail_block = jnp.where(seq_index == seq_count - 1, glob_out[BLK:], attended)
    attended = attended.at[tokens - BLK :].set(tail_block)
    partial_terms = lax.dot_general(
        lax.all_gather(out_weight, "seq", axis=0, tiled=True),
        attended,
        (((1,), (1,)), ((), ())),
        preferred_element_type=jnp.float32,
    )
    summed = lax.psum_scatter(
        partial_terms.astype(jnp.bfloat16), "head", scatter_dimension=0, tiled=True
    ).astype(jnp.float32)
    return summed.T.astype(jnp.bfloat16)


def spread_kernel(head, seq_ref, query_ref, key_ref, value_ref, *out_refs):
    heads = value_ref.shape[1] // HD // PEERS
    for apart, out_ref in enumerate(out_refs):
        start = ((seq_ref[0] ^ apart) * heads + head) * HD
        lanes = pl.ds(pl.multiple_of(start, HD), HD)
        for which, ref in enumerate((query_ref, key_ref, value_ref)):
            out_ref[which] = ref[:, lanes]


def spread(seq_index, query_rows, key_rows, value_rows, head):
    tokens, features = query_rows.shape
    piece = jax.ShapeDtypeStruct((3, tokens, HD), query_rows.dtype)
    whole = pl.BlockSpec((tokens, features), lambda i: (0, 0))
    return pl.pallas_call(
        functools.partial(spread_kernel, head),
        grid=(1,),
        in_specs=[SCALARS] + [whole] * 3,
        out_specs=[pl.BlockSpec(piece.shape, lambda i: (0, 0, 0))] * PEERS,
        out_shape=[piece] * PEERS,
        cost_estimate=pl.CostEstimate(
            flops=0, bytes_accessed=12 * tokens * features, transcendentals=0
        ),
    )(seq_index[None], query_rows, key_rows, value_rows)


def attend_kernel(head, seq_ref, bias_ref, *refs):
    *pieces, out_ref = refs
    tokens = pieces[0].shape[1]
    factor = math.log2(math.e) / math.sqrt(HD)
    keys = jnp.concatenate([piece[1] for piece in pieces], axis=0)
    values = jnp.concatenate([piece[2] for piece in pieces], axis=0)
    for apart, piece in enumerate(pieces):
        scores = lax.dot_general(
            piece[0], keys, (((1,), (1,)), ((), ())), preferred_element_type=jnp.float32
        )
        scores = scores * factor + bias_ref[head, apart : apart + 1, :]
        peak = jnp.max(scores, axis=1, keepdims=True)
        terms = jnp.exp2(scores - peak)
        denom = jnp.sum(terms, axis=1, keepdims=True)
        mixed = jnp.dot(
            terms.astype(jnp.bfloat16), values, preferred_element_type=jnp.float32
        )
        rows = pl.ds(pl.multiple_of((seq_ref[0] ^ apart) * tokens, tokens), tokens)
        out_ref[rows, :] = (mixed / denom).astype(out_ref.dtype)


def attend_head(seq_index, bias, pieces, head):
    _, tokens, width = pieces[0].shape
    total = len(pieces) * tokens
    return pl.pallas_call(
        functools.partial(attend_kernel, head),
        in_specs=[SCALARS] + [ARRAY] * (1 + len(pieces)),
        out_shape=jax.ShapeDtypeStruct((total, width), pieces[0].dtype),
        compiler_params=pltpu.CompilerParams(vmem_limit_bytes=VMEM),
        cost_estimate=pl.CostEstimate(
            flops=4 * total * total * width,
            bytes_accessed=8 * total * width,
            transcendentals=total * total,
        ),
    )(seq_index[None], bias, *pieces)


def product_tile(owner_ref, pieces, weight_ref, tile):
    heads = len(pieces) // owner_ref.shape[0]
    width = heads * HD
    rows = jnp.concatenate([piece[tile, :] for piece in pieces], axis=1)
    columns = [
        weight_ref[:, pl.ds(pl.multiple_of(owner_ref[k] * width, width), width)]
        for k in range(owner_ref.shape[0])
    ]
    return lax.dot_general(
        rows,
        jnp.concatenate(columns, axis=1),
        (((1,), (1,)), ((), ())),
        preferred_element_type=jnp.float32,
    )


def early_kernel(owner_ref, weight_ref, *refs):
    *pieces, total_ref = refs
    for start in range(0, total_ref.shape[0], TILE):
        tile = slice(start, start + TILE)
        total_ref[tile, :] = product_tile(owner_ref, pieces, weight_ref, tile)


def late_kernel(owner_ref, side_ref, weight_ref, total_ref, *refs):
    *pieces, out_ref = refs
    half = out_ref.shape[1]
    outs = pl.ds(pl.multiple_of(side_ref[0] * half, half), half)
    for start in range(0, total_ref.shape[0], TILE):
        tile = slice(start, start + TILE)
        product = product_tile(owner_ref, pieces, weight_ref.at[outs, :], tile)
        out_ref[tile, :] = (total_ref[tile, outs] + product).astype(out_ref.dtype)


def project_early(owners, pieces, weight):
    total, width = pieces[0].shape
    outs = weight.shape[0]
    return pl.pallas_call(
        early_kernel,
        in_specs=[SCALARS] + [ARRAY] * (1 + len(pieces)),
        out_shape=jax.ShapeDtypeStruct((total, outs), jnp.float32),
        compiler_params=pltpu.CompilerParams(vmem_limit_bytes=VMEM),
        cost_estimate=pl.CostEstimate(
            flops=2 * total * outs * width * len(pieces),
            bytes_accessed=2 * len(pieces) * width * (total + outs) + 4 * total * outs,
            transcendentals=0,
        ),
    )(owners, weight, *pieces)


def project_late(owners, side, pieces, weight, so_far):
    total, width = pieces[0].shape
    outs = weight.shape[0]
    return pl.pallas_call(
        late_kernel,
        in_specs=[SCALARS] * 2 + [ARRAY] * (2 + len(pieces)),
        out_shape=jax.ShapeDtypeStruct((total, outs // 2), pieces[0].dtype),
        compiler_params=pltpu.CompilerParams(vmem_limit_bytes=VMEM),
        cost_estimate=pl.CostEstimate(
            flops=total * outs * width * len(pieces),
            bytes_accessed=2 * len(pieces) * width * (total + outs) + 6 * total * outs,
            transcendentals=0,
        ),
    )(owners, side, weight, so_far, *pieces)


def add_kernel(row_ref, keep_ref, other_ref, *out_refs):
    tokens = out_refs[0].shape[0]
    for apart, out_ref in enumerate(out_refs):
        rows = pl.ds(pl.multiple_of((row_ref[0] ^ apart) * tokens, tokens), tokens)
        out_ref[...] = (
            keep_ref[rows, :].astype(jnp.float32) + other_ref[rows, :].astype(jnp.float32)
        ).astype(out_ref.dtype)


def add_and_part(row, keep, other, parts):
    total, width = keep.shape
    return pl.pallas_call(
        add_kernel,
        in_specs=[SCALARS] + [ARRAY] * 2,
        out_shape=[jax.ShapeDtypeStruct((total // parts, width), keep.dtype)] * parts,
        compiler_params=pltpu.CompilerParams(vmem_limit_bytes=VMEM),
        cost_estimate=pl.CostEstimate(
            flops=total * width, bytes_accessed=6 * total * width, transcendentals=0
        ),
    )(row[None], keep, other)


def assemble_kernel(seq_ref, head_ref, near_ref, crossed_ref, *refs):
    *arrived, out_ref = refs
    reach = len(arrived) // 2
    width = arrived[0].shape[1]
    near = near_ref[0] == 1
    for i in range(reach):
        spot = 2 * ((seq_ref[0] % reach) ^ i)
        mine = pl.ds(pl.multiple_of((spot + head_ref[0]) * width, width), width)
        theirs = pl.ds(pl.multiple_of((spot + 1 - head_ref[0]) * width, width), width)
        out_ref[:, mine] = jnp.where(near, arrived[i][...], arrived[i + reach][...])
        out_ref[:, theirs] = crossed_ref[i]


def assemble(seq_index, head_index, near, crossed, arrived):
    tokens, width = arrived[0].shape
    return pl.pallas_call(
        assemble_kernel,
        in_specs=[SCALARS] * 3 + [ARRAY] * (1 + len(arrived)),
        out_shape=jax.ShapeDtypeStruct((tokens, width * len(arrived)), crossed.dtype),
        compiler_params=pltpu.CompilerParams(vmem_limit_bytes=VMEM),
    )(seq_index[None], head_index[None], near[None], crossed, *arrived)


def key_bias(rand_blocks, seq_index, head_start, heads):
    block_total = rand_blocks.shape[0]
    ids = seq_index ^ jnp.arange(block_total, dtype=jnp.int32)
    near = jnp.abs(ids[:, None] - ids[None, :]) <= 1
    ends = (ids == 0) | (ids == block_total - 1)
    fixed = near | ends[None, :] | ends[:, None]
    chosen = lax.dynamic_slice_in_dim(rand_blocks, head_start, heads, 1)[ids]
    named = jnp.any(chosen[:, :, :, None] == ids, axis=2).transpose(1, 0, 2)
    live = named | fixed[None]
    return jnp.repeat(jnp.where(live, 0.0, -1e30).astype(jnp.float32), BLK, axis=2)


def ring_order(peers):
    return list(range(0, peers, 2)) + list(range(peers - 1, 0, -2))


def local_by_heads(query_rows, key_rows, value_rows, rand_blocks, out_weight):
    tokens, features = query_rows.shape
    peers = lax.axis_size("seq")
    seq_index = lax.axis_index("seq")
    head_index = lax.axis_index("head")
    heads = features // HD // peers
    order = ring_order(peers)
    onward = [(order[i], order[(i + 1) % peers]) for i in range(peers)]
    back = [(target, source) for source, target in onward]
    outgoing = []
    for head in range(heads):
        if head:
            query_rows, _ = lax.optimization_barrier((query_rows, outgoing[0]))
        outgoing += spread(seq_index, query_rows, key_rows, value_rows, head)
    bias = key_bias(rand_blocks, seq_index, head_index * (features // HD) + seq_index * heads, heads)
    reach = peers // 2
    far = {}
    pieces = {}
    for head in range(heads):
        pieces[head, 0] = outgoing[head * peers]
        for spot, apart in enumerate(ROWS_ORDER[head % 2]):
            if head and spot >= len(ROWS_ORDER[0]) - HELD:
                continue
            pairs = [(i, i ^ apart) for i in range(peers)]
            pieces[head, apart] = lax.ppermute(outgoing[head * peers + apart], "seq", pairs)
    for head in range(heads):
        if head:
            for apart in ROWS_ORDER[head % 2][len(ROWS_ORDER[0]) - HELD :]:
                pairs = [(i, i ^ apart) for i in range(peers)]
                piece, _ = lax.optimization_barrier((outgoing[head * peers + apart], far[0, 0]))
                pieces[head, apart] = lax.ppermute(piece, "seq", pairs)
        group = [pieces[head, apart] for apart in range(peers)]
        if head and EARLY_STEPS:
            held = [far[0, 1], far[0, -1]][:EARLY_STEPS]
            *group, = lax.optimization_barrier((*group, *held))[:peers]
        mine = attend_head(seq_index, bias, group, head)
        ahead, behind = (mine, mine)
        far[head, 0] = mine
        for step in range(1, reach):
            ahead = lax.ppermute(ahead, "seq", onward)
            behind = lax.ppermute(behind, "seq", back)
            far[head, step] = ahead
            far[head, -step] = behind
        if head % 2 == 0:
            far[head, reach] = lax.ppermute(ahead, "seq", onward)
        else:
            far[head, reach] = lax.ppermute(behind, "seq", back)
    place = jnp.where(seq_index % 2 == 0, seq_index // 2, peers - (seq_index + 1) // 2)

    def gather_args(steps):
        spots = (place - jnp.array(steps, jnp.int32)) % peers
        owners = jnp.where(spots < reach, 2 * spots, 2 * (peers - spots) - 1)
        return owners, [far[head, step] for step in steps for head in range(heads)]

    steps = [0] + [step for hop in range(1, reach) for step in (hop, -hop)] + [reach]
    owners, pieces = gather_args(steps[:EARLY])
    so_far = project_early(owners, pieces, out_weight)
    owners, pieces = gather_args(steps[EARLY:])
    send = project_late(owners, 1 - head_index[None], pieces, out_weight, so_far)
    swap = [(0, 1), (1, 0)]
    other = lax.ppermute(send, "head", swap)
    keep = project_late(owners, head_index[None], pieces, out_weight, so_far)
    parts = add_and_part(seq_index, keep, other, peers)
    arrived = {0: parts[0]}
    for apart in SEND_ORDER:
        pairs = [(i, i ^ apart) for i in range(peers)]
        arrived[apart] = lax.ppermute(parts[apart], "seq", pairs)
    near = (seq_index // reach == head_index).astype(jnp.int32)
    theirs = [jnp.where(near == 1, arrived[i + reach], arrived[i]) for i in range(reach)]
    crossed = lax.ppermute(jnp.stack(theirs), "head", swap)
    return assemble(seq_index, head_index, near, crossed, [arrived[i] for i in range(peers)])


def local(query_rows, key_rows, value_rows, rand_blocks, out_weight):
    tokens, features = query_rows.shape
    peers = lax.axis_size("seq")
    even = features // HD % peers == 0
    if tokens == BLK and peers == PEERS and lax.axis_size("head") == 2 and even:
        return local_by_heads(query_rows, key_rows, value_rows, rand_blocks, out_weight)
    return local_by_rows(query_rows, key_rows, value_rows, rand_blocks, out_weight)


def solution(mesh):
    placed = (
        P(("rep", "seq"), "head"),
        P(("rep", "seq"), "head"),
        P(("rep", "seq"), "head"),
        P("rep", None, None),
        P("seq", "head"),
    )
    return jax.shard_map(
        local, mesh=mesh, in_specs=placed, out_specs=P(("rep", "seq"), "head"), check_vma=False
    )
```
